32 devices in a mesh: row: 4 (over z), col: 4 (over y, core), depth: 2 (over x).
Axes of the slice: x: 2, y: 2, z: 4, core: 2. Of those that a mesh axis runs over, the one named last changes fastest.
Arguments:
- tokens: bfloat16 [256, 12288], P(('row', 'col'), 'depth'), may hold values from -6 to 6
- in_weight: bfloat16 [12288, 49152], P('depth', ('row', 'col')), may hold values from -0.0546875 to 0.0546875
- in_bias: bfloat16 [49152], P(('row', 'col')), may hold values from -4 to 4
- out_weight: bfloat16 [49152, 12288], P(('row', 'col'), 'depth'), may hold values from -0.02734375 to 0.02734375
- out_bias: bfloat16 [12288], P('depth'), may hold values from -3 to 3
Outputs:
- outputs: bfloat16 [256, 12288], P(('row', 'col'), 'depth')
The draws below stay inside these ranges and needn't reach their ends.
All inputs are finite; a program needn't handle non-finite values.
Results may differ from the reference program's by a relative error of at most 0.0045.
Values may be sent and summed in bfloat16 or wider, within the bound.
A program may use at most 192 MiB of HBM per device.

```python
import jax
import jax.numpy as jnp

D = 12288
FF = 49152
TOKENS = 256


def shard_levels(own_key, extent, split, least, top_value):
    def one(dim, shards_of):
        draws = jax.random.uniform(jax.random.fold_in(jax.random.fold_in(own_key, 6), dim), (shards_of,), jnp.float32, least / len(split), top_value / len(split))
        return jnp.repeat(jnp.exp(draws), extent[dim] // shards_of).reshape((-1,) + (1,) * (len(extent) - dim - 1))

    gain = one(*split[0])
    for cut in split[1:]:
        gain = gain * one(*cut)
    return gain


def scatter_about(rng, shape, width, reach, cuts=(), dtype=jnp.bfloat16):
    gain = shard_levels(rng, shape, cuts, -0.22, 0.18) if cuts else 1.0
    entries = jax.random.normal(rng, shape, jnp.float32) * width * gain
    return jnp.minimum(jnp.maximum(entries, -reach), reach).astype(dtype)


def setup_inputs(seed: int = 0) -> dict:
    keys = jax.random.split(jax.random.key(seed), 6)
    tokens = scatter_about(keys[0], (TOKENS, D), 1.0, 6.0, ((0, 16), (1, 2)))
    in_weight = scatter_about(keys[1], (D, FF), D ** -0.5, 0.0546875, ((0, 2), (1, 16)))
    in_bias = scatter_about(keys[2], (FF,), 1.0, 4.0, ((0, 16),))
    out_weight = scatter_about(keys[3], (FF, D), FF ** -0.5, 0.02734375, ((0, 16), (1, 2)))
    out_bias = scatter_about(keys[4], (D,), 0.5, 3.0, ((0, 2),))
    return {"tokens": tokens, "in_weight": in_weight, "in_bias": in_bias, "out_weight": out_weight, "out_bias": out_bias}


def reference(tokens, in_weight, in_bias, out_weight, out_bias):
    pre = jnp.dot(tokens, in_weight, preferred_element_type=jnp.float32) + in_bias.astype(jnp.float32)
    hidden = jax.nn.gelu(pre, approximate=True).astype(jnp.bfloat16)
    summed = jnp.dot(hidden, out_weight, preferred_element_type=jnp.float32) + out_bias.astype(jnp.float32)
    return summed.astype(jnp.bfloat16)
```

```python
import functools

import jax
import jax.numpy as jnp
from jax import lax
from jax.experimental import pallas as pl
from jax.experimental.pallas import tpu as pltpu
from jax.sharding import PartitionSpec as P

CORES = 2
BF16 = jnp.bfloat16
F32 = jnp.float32


def partner(i, step, n):
    if n & (n - 1):
        return (i + step) % n
    out, bit = 0, 1
    while bit < n:
        own = i // bit % 2
        out = out + bit * (1 - own if step & bit else own)
        bit *= 2
    return out


def general_kernel(
    R, C, DP, tps, nch, nb, ch,
    x_ref, w1_ref, b1_ref, w2_ref, b2_ref, out_ref,
    xbuf, slots, own, psend, precv, hbuf, acc, s1s, s1r, s2s, s2r, own2, s3s, s3r,
    w1_sem, w2_sem, ag_ss, ag_rs, p_ss, p_rs, s1_ss, s1_rs, s2_ss, s2_rs, s3_ss, s3_rs,
):
    Y = C // CORES
    z = lax.axis_index("row")
    col = lax.axis_index("col")
    dp = lax.axis_index("depth")
    y = col // CORES
    c = col % CORES
    sib = y * CORES + (1 - c)

    def remote(src, dst, ss, rs, **dev):
        return pltpu.make_async_remote_copy(
            src_ref=src, dst_ref=dst, send_sem=ss, recv_sem=rs,
            device_id=dev, device_id_type=pl.DeviceIdType.MESH,
        )

    def w1_copy(k):
        return pltpu.make_async_copy(w1_ref.at[:, pl.ds(pl.multiple_of(k * ch, ch), ch)], slots.at[k], w1_sem.at[k])

    ffl = w2_ref.shape[0]
    per = nb // nch

    def w2_slot(n):
        return n // per, pl.ds(pl.multiple_of(n % per * ffl, ffl), ffl)

    def w2_copy(n):
        return pltpu.make_async_copy(
            w2_ref.at[:, pl.ds(pl.multiple_of(n * ch, ch), ch)], slots.at[w2_slot(n)], w2_sem.at[n]
        )

    @pl.loop(0, nch)
    def _(k):
        w1_copy(k).start()

    barrier = pltpu.get_barrier_semaphore()

    def greet(**dev):
        pl.semaphore_signal(barrier, inc=1, device_id=dev, device_id_type=pl.DeviceIdType.MESH)

    z_peers = [partner(z, dz, R) for dz in range(1, R)]
    chain = R == 4
    far = 1 - z // (R // 2)
    if chain:
        z_order = [z, partner(z, 1, R), 1 + far, 3 * far]
        across = 3 - z
        inner = (z == 1) | (z == 2)
    else:
        z_order = [z] + z_peers
    y_peers = [(y + dy) % Y for dy in range(1, Y)]
    d_peers = [(dp + dd) % DP for dd in range(1, DP)]
    for zt in z_peers:
        greet(row=zt)
    for yt in y_peers:
        greet(col=yt * CORES + c)
    greet(col=sib)
    for dt in d_peers:
        greet(depth=dt)

    def shard(zz, yy, cc):
        return zz * C + yy * CORES + cc

    def rows(s):
        return pl.ds(pl.multiple_of(s * tps, tps), tps)

    me = shard(z, y, c)
    xbuf[rows(me)] = x_ref[...]
    pl.semaphore_wait(barrier, (R - 1) + (Y - 1) + 1 + (DP - 1))

    sent = []

    def send_shard(s, inner_only=False, **dev):
        copy = remote(xbuf.at[rows(s)], xbuf.at[rows(s)], ag_ss.at[len(sent)], ag_rs.at[s], **dev)
        sent.append((copy, inner_only))
        if inner_only:
            pl.when(inner)(copy.start)
        else:
            copy.start()

    def await_shard(s):
        remote(xbuf.at[rows(s)], xbuf.at[rows(s)], ag_ss.at[0], ag_rs.at[s], col=sib).wait_recv()

    if chain:
        send_shard(me, inner_only=True, row=across)
        send_shard(me, row=z_order[1])
    else:
        for zt in z_peers:
            send_shard(me, row=zt)
    for yt in y_peers:
        send_shard(me, col=yt * CORES + c)
    send_shard(me, col=sib)

    def forward_z(i):
        s = shard(z_order[i], y, c)
        await_shard(s)
        if chain:
            send_shard(s, inner_only=True, row=across if i == 1 else z_order[1])
        for yt in y_peers:
            send_shard(s, col=yt * CORES + c)
        send_shard(s, col=sib)

    def forward_y(i):
        for yt in y_peers:
            s = shard(z_order[i], yt, c)
            await_shard(s)
            send_shard(s, col=sib)

    half = R // 2

    def block_rows(b):
        size = half * C * tps
        return pl.ds(pl.multiple_of((1 - far if b == 0 else far) * size, size), size)

    def p_copy(i, k, b):
        r = block_rows(b)
        return remote(
            psend.at[k, r], precv.at[i, k, r], p_ss.at[i, k, b], p_rs.at[i, k, b], depth=d_peers[i]
        )

    def project(b, first, last):
        r = block_rows(b)

        @pl.loop(first, last)
        def _(k):
            if b == 0:
                w1_copy(k).wait()
            partial = jnp.dot(xbuf[r], slots[k], preferred_element_type=F32)
            own[k, r] = partial
            psend[k, r] = partial.astype(BF16)
            for i in range(DP - 1):
                p_copy(i, k, b).start()
            if b == 1:
                for j in range(per):
                    w2_copy(k * per + j).start()

    def await_block(b):
        for i in range(b * half, (b + 1) * half):
            for yt in [y] + y_peers:
                await_shard(shard(z_order[i], yt, 1 - c))

    for i in range(1, half):
        forward_z(i)
    for i in range(half):
        forward_y(i)
    forward_z(half)
    await_block(0)
    cut1, cut2 = nch // 3, 2 * nch // 3
    project(0, 0, cut1)
    for i in range(half + 1, R):
        forward_z(i)
    forward_y(half)
    project(0, cut1, cut2)
    for i in range(half + 1, R):
        forward_y(i)
    project(0, cut2, nch)
    await_block(1)
    project(1, 0, nch)

    def hidden(k):
        for i in range(DP - 1):
            for b in range(2):
                p_copy(i, k, b).wait_recv()
        pre = own[k]
        for i in range(DP - 1):
            pre = pre + precv[i, k].astype(F32)
        cols = pl.ds(pl.multiple_of(k * ch, ch), ch)
        pre = pre + b1_ref[:, cols].astype(F32)
        hbuf[:, cols] = jax.nn.gelu(pre, approximate=True).astype(BF16)

    def multiply(n):
        w2_copy(n).wait()
        acc[n] = jnp.dot(hbuf[...], slots[w2_slot(n)], preferred_element_type=F32)

    pl.loop(0, nch)(hidden)

    def s1_copy(n):
        return remote(s1s.at[n], s1r.at[n], s1_ss.at[n], s1_rs.at[n], col=sib)

    def s2_copy(i, n):
        return remote(s2s.at[i, n], s2r.at[i, n], s2_ss.at[i, n], s2_rs.at[i, n], col=y_peers[i] * CORES + c)

    def s3_copy(i, n):
        return remote(s3s.at[i, n], s3r.at[i, n], s3_ss.at[i, n], s3_rs.at[i, n], row=z_peers[i])

    def stage2(n):
        s1_copy(n).wait_recv()

        def chip_sum(j):
            return acc[n, rows(CORES * j + c)] + s1r[n, rows(j)].astype(F32)

        for i, yt in enumerate(y_peers):
            for zz in range(R):
                s2s[i, n, rows(zz)] = chip_sum(zz * Y + yt).astype(BF16)
            s2_copy(i, n).start()
        for zz in range(R):
            own2[n, rows(zz)] = chip_sum(zz * Y + y)

    @pl.loop(0, nb)
    def _(n):
        multiply(n)
        for j in range(R * Y):
            s1s[n, rows(j)] = acc[n, rows(CORES * j + 1 - c)].astype(BF16)
        s1_copy(n).start()

        @pl.when(n > 0)
        def _():
            stage2(n - 1)

    stage2(nb - 1)

    @pl.loop(0, nb)
    def _(n):
        total = own2[n]
        for i in range(Y - 1):
            s2_copy(i, n).wait_recv()
        for i in range(Y - 1):
            total = total + s2r[i, n].astype(F32)
        own2[n] = total
        for i, zt in enumerate(z_peers):
            s3s[i, n] = own2[n, rows(zt)].astype(BF16)
            s3_copy(i, n).start()

    @pl.loop(0, nb)
    def _(n):
        cols = pl.ds(pl.multiple_of(n * ch, ch), ch)
        for i in range(R - 1):
            s3_copy(i, n).wait_recv()
        total = own2[n, rows(z)]
        for i in range(R - 1):
            total = total + s3r[i, n].astype(F32)
        out_ref[:, cols] = (total + b2_ref[:, cols].astype(F32)).astype(BF16)

    for copy, inner_only in sent:
        if inner_only:
            pl.when(inner)(copy.wait_send)
        else:
            copy.wait_send()

    @pl.loop(0, nch)
    def _(k):
        for i in range(DP - 1):
            for b in range(2):
                p_copy(i, k, b).wait_send()

    @pl.loop(0, nb)
    def _(n):
        s1_copy(n).wait_send()
        for i in range(Y - 1):
            s2_copy(i, n).wait_send()
        for i in range(R - 1):
            s3_copy(i, n).wait_send()


def grid_kernel(
    tps, ch, half,
    x_ref, w1_ref, b1_ref, w2_ref, b2_ref, out_ref,
    xbuf, slots, own, psend, precv, hbuf, b1v, b2v, acc, s1s, s1r, s2s, s2r, own2, s3s, s3r, s4s, s4r,
    in_sem, w1_sem, w2_sem, ag_ss, ag_rs, p_ss, p_rs, s1_ss, s1_rs, s2_ss, s2_rs, s3_ss, s3_rs, s4_ss, s4_rs, far_sem,
):
    unit = CORES * tps
    ffl, dl = w2_ref.shape
    nch, nb = ffl // ch, dl // ch
    per = nb // nch
    z = lax.axis_index("row")
    col = lax.axis_index("col")
    dp = lax.axis_index("depth")
    y = col // CORES
    c = col % CORES
    top = z // 2
    inner = (z == 1) | (z == 2)
    end = jnp.logical_not(inner)
    SIB = {"col": y * CORES + (1 - c)}
    YN = {"col": (1 - y) * CORES + c}
    ZN = {"row": z + 1 - 2 * (z % 2)}
    ACROSS = {"row": 3 - z}
    FAR = {"row": 3 * (1 - top)}
    XN = {"depth": 1 - dp}

    def remote(src, dst, ss, rs, dev):
        return pltpu.make_async_remote_copy(
            src_ref=src, dst_ref=dst, send_sem=ss, recv_sem=rs,
            device_id=dev, device_id_type=pl.DeviceIdType.MESH,
        )

    barrier = pltpu.get_barrier_semaphore()

    def signal(sem, dev):
        pl.semaphore_signal(sem, inc=1, device_id=dev, device_id_type=pl.DeviceIdType.MESH)

    for dev in (XN, YN, ZN, SIB):
        signal(barrier, dev)
    pl.when(inner)(lambda: signal(barrier, ACROSS))

    def colsof(k, n=1):
        return pl.ds(pl.multiple_of(k * ch, ch), n * ch)

    x_copy = pltpu.make_async_copy(x_ref, xbuf.at[pl.ds(0, tps)], in_sem.at[0])
    b1_copy = pltpu.make_async_copy(b1_ref, b1v, in_sem.at[1])
    b2_copy = pltpu.make_async_copy(b2_ref, b2v, in_sem.at[2])
    x_copy.start()

    def w1_copy(k):
        return pltpu.make_async_copy(w1_ref.at[:, colsof(k)], slots.at[k], w1_sem.at[k])

    def w2_slot(n):
        return n // per, pl.ds(pl.multiple_of(n % per * ffl, ffl), ffl)

    def w2_copy(n):
        return pltpu.make_async_copy(w2_ref.at[:, colsof(n)], slots.at[w2_slot(n)], w2_sem.at[n])

    @pl.loop(0, nch)
    def _(k):
        w1_copy(k).start()

    b1_copy.start()
    b2_copy.start()
    x_copy.wait()
    pl.semaphore_wait(barrier, 4 + (z % 3 + 1) // 2)

    def part(slot, rel):
        return pl.ds(slot * unit + rel * tps, tps)

    sent = []

    def send(src, dst, dev, only=None):
        copy = remote(xbuf.at[part(*src)], xbuf.at[part(*dst)], ag_ss.at[len(sent)], ag_rs.at[2 * dst[0] + dst[1]], dev)
        sent.append((copy, only))
        if only is None:
            copy.start()
        else:
            pl.when(only)(copy.start)

    def landed(slot, rel):
        remote(xbuf.at[part(slot, rel)], xbuf.at[part(slot, rel)], ag_ss.at[0], ag_rs.at[2 * slot + rel], SIB).wait_recv()

    send((0, 0), (0, 1), SIB)
    send((0, 0), (2, 0), ZN)
    send((0, 0), (4, 0), ACROSS, inner)
    send((0, 0), (1, 0), YN)
    pl.when(inner)(lambda: signal(far_sem, ACROSS))

    def p_copy(kind, r0, nr, k):
        at = (pl.ds(r0, nr), colsof(k))
        return remote(psend.at[at], precv.at[at], p_ss.at[kind, k], p_rs.at[kind, k], XN)

    def project(kind, r0, nr, k):
        rows = pl.ds(r0, nr)
        partial = jnp.dot(xbuf[rows], slots[k], preferred_element_type=F32)
        own[rows, colsof(k)] = partial
        psend[rows, colsof(k)] = partial.astype(BF16)
        p_copy(kind, r0, nr, k).start()

    def hidden(r0, nr, k):
        at = (pl.ds(r0, nr), colsof(k))
        pre = own[at] + precv[at].astype(F32) + b1v[:, colsof(k)].astype(F32)
        hbuf[at] = jax.nn.gelu(pre, approximate=True).astype(BF16)

    early = 2 * nch // 3
    A = (0, 0, unit)
    B = (1, unit, 2 * unit)
    AB = (0, 0, 3 * unit)
    C = (2, 3 * unit, 3 * unit)
    D = (3, 6 * unit, 2 * unit)

    landed(0, 1)

    @pl.loop(0, early)
    def _(k):
        w1_copy(k).wait()
        project(*A, k)

    landed(2, 0)
    send((2, 0), (6, 0), ACROSS, inner)
    send((2, 0), (3, 0), YN)
    send((2, 0), (2, 1), SIB)
    landed(1, 0)
    send((1, 0), (1, 1), SIB)

    def relay(slot, only):
        pl.when(only)(lambda: landed(slot, 0))
        send((slot, 0), (slot, 0), ZN, inner if only is inner else None) if only is inner else None
        send((slot, 0), (slot + 1, 0), YN, only)
        send((slot, 0), (slot, 1), SIB, only)

    relay(4, inner)
    landed(2, 1)
    landed(1, 1)

    @pl.loop(0, early)
    def _(k):
        project(*B, k)

    landed(3, 0)
    send((3, 0), (3, 1), SIB)
    relay(4, end)
    relay(6, inner)

    @pl.loop(early, nch)
    def _(k):
        w1_copy(k).wait()
        project(*AB, k)

    landed(5, 0)
    send((5, 0), (5, 1), SIB)
    relay(6, end)
    for slot in (3, 4, 5):
        landed(slot, 1)

    @pl.loop(0, nch)
    def _(k):
        project(*C, k)

    landed(7, 0)
    send((7, 0), (7, 1), SIB)
    landed(6, 1)
    landed(7, 1)
    b1_copy.wait()
    b2_copy.wait()

    def ab_arrived(k):
        @pl.when(k < early)
        def _():
            p_copy(*A, k).wait_recv()
            p_copy(*B, k).wait_recv()

        @pl.when(k >= early)
        def _():
            p_copy(*AB, k).wait_recv()

    @pl.loop(0, nch)
    def _(k):
        ab_arrived(k)
        project(*D, k)
        hidden(0, 3 * unit, k)
        for j in range(per):
            w2_copy(k * per + j).start()

    @pl.loop(0, nch)
    def _(k):
        p_copy(*C, k).wait_recv()
        hidden(3 * unit, 3 * unit, k)

    PASSES = ((0, 6), (6, 2))

    def sub(first, count):
        return pl.ds(first * tps, count * tps)

    def s1_copy(p, n):
        at = (n, sub(*PASSES[p]))
        return remote(s1s.at[at], s1r.at[at], s1_ss.at[p, n], s1_rs.at[p, n], SIB)

    def s2_copy(p, n):
        at = (n, sub(PASSES[p][0] // 2, PASSES[p][1] // 2))
        return remote(s2s.at[at], s2r.at[at], s2_ss.at[p, n], s2_rs.at[p, n], YN)

    def s3_copy(i, n):
        return remote(s3s.at[n, sub(i, 1)], s3r.at[n, sub(i, 1)], s3_ss.at[i, n], s3_rs.at[i, n], ZN)

    def s4_copy(p, n):
        return remote(s4s.at[n, sub(p, 1)], s4r.at[n], s4_ss.at[p, n], s4_rs.at[n], FAR if p else ACROSS)

    def multiply(p, n):
        first, count = PASSES[p]
        if p == 0:
            w2_copy(n).wait()
        prod = jnp.dot(hbuf[pl.ds(first * unit, count * unit)], slots[w2_slot(n)], preferred_element_type=F32)
        for j in range(count):
            acc[n, sub(first + j, 1)] = prod[j * unit : j * unit + tps]
            s1s[n, sub(first + j, 1)] = prod[j * unit + tps : (j + 1) * unit].astype(BF16)
        s1_copy(p, n).start()

    def stage2(p, n):
        first, count = PASSES[p]
        s1_copy(p, n).wait_recv()
        for j in range(first, first + count):
            total = acc[n, sub(j, 1)] + s1r[n, sub(j, 1)].astype(F32)
            if j % 2:
                s2s[n, sub(j // 2, 1)] = total.astype(BF16)
            else:
                own2[n, sub(j // 2, 1)] = total
        s2_copy(p, n).start()

    def stage3(p, n):
        first, count = PASSES[p]
        s2_copy(p, n).wait_recv()
        for j in range(first // 2, (first + count) // 2):
            total = own2[n, sub(j, 1)] + s2r[n, sub(j, 1)].astype(F32)
            own2[n, sub(j, 1)] = total
            if j == 1:
                s3s[n, sub(0, 1)] = total.astype(BF16)
                s3_copy(0, n).start()
            elif j > 1:
                @pl.when(end)
                def _():
                    s3s[n, sub(1 + p, 1)] = total.astype(BF16)
                    s3_copy(1 + p, n).start()

    def stage4(p, n):
        if p == 0:
            s3_copy(0, n).wait_recv()
            own2[n, sub(0, 1)] = own2[n, sub(0, 1)] + s3r[n, sub(0, 1)].astype(F32)

        @pl.when(inner)
        def _():
            s3_copy(1 + p, n).wait_recv()
            total = own2[n, sub(2 + p, 1)] + s3r[n, sub(1 + p, 1)].astype(F32)
            s4s[n, sub(p, 1)] = total.astype(BF16)
            s4_copy(p, n).start()

    def finish(n):
        s4_copy(0, n).wait_recv()
        total = own2[n, sub(0, 1)] + s4r[n].astype(F32)
        out_ref[:, colsof(n)] = (total + b2v[:, colsof(n)].astype(F32)).astype(BF16)

    def at(first, last, step, fn, *args):
        pl.when((step >= first) & (step < last))(lambda: fn(*args))

    @pl.loop(0, nb)
    def _(n):
        multiply(0, n)
        at(1, nb, n, stage2, 0, n - 1)
        at(half, nb, n, stage3, 0, n - half)
        at(half + 2, nb, n, stage4, 0, n - half - 2)

    stage2(0, nb - 1)

    @pl.loop(0, nch)
    def _(k):
        p_copy(*D, k).wait_recv()
        hidden(6 * unit, 2 * unit, k)

    pl.when(inner)(lambda: pl.semaphore_wait(far_sem, 1))

    @pl.loop(0, nb)
    def _(n):
        multiply(1, n)
        at(1, nb, n, stage2, 1, n - 1)
        at(0, half, n, stage3, 0, n + nb - half)
        at(0, half + 2, n, stage4, 0, n + nb - half - 2)
        at(half, nb, n, stage3, 1, n - half)
        at(half + 2, nb, n, stage4, 1, n - half - 2)

    stage2(1, nb - 1)

    @pl.loop(nb - half, nb)
    def _(n):
        stage3(1, n)

        stage4(1, n - 2)

    stage4(1, nb - 2)
    stage4(1, nb - 1)
    pl.loop(0, nb)(finish)

    for copy, only in sent:
        if only is None:
            copy.wait_send()
        else:
            pl.when(only)(copy.wait_send)

    @pl.loop(0, nch)
    def _(k):
        @pl.when(k < early)
        def _():
            p_copy(*A, k).wait_send()
            p_copy(*B, k).wait_send()

        @pl.when(k >= early)
        def _():
            p_copy(*AB, k).wait_send()

        p_copy(*C, k).wait_send()
        p_copy(*D, k).wait_send()

    @pl.loop(0, nb)
    def _(n):
        for p in range(2):
            s1_copy(p, n).wait_send()
            s2_copy(p, n).wait_send()
        s3_copy(0, n).wait_send()

        @pl.when(end)
        def _():
            s3_copy(1, n).wait_send()
            s3_copy(2, n).wait_send()

        @pl.when(inner)
        def _():
            s4_copy(0, n).wait_send()
            s4_copy(1, n).wait_send()


def grid_call(tokens, in_weight, in_bias, out_weight, out_bias):
    tps, dl = tokens.shape
    ffl = in_weight.shape[1]
    T = 16 * tps
    ch = 512
    half = 4
    nch, nb = ffl // ch, dl // ch
    vmem = pl.BlockSpec(memory_space=pltpu.VMEM)
    hbm = pl.BlockSpec(memory_space=pl.ANY)
    dma = pltpu.SemaphoreType.DMA
    return pl.pallas_call(
        functools.partial(grid_kernel, tps, ch, half),
        out_shape=jax.ShapeDtypeStruct((tps, dl), BF16),
        in_specs=[hbm] * 5,
        out_specs=vmem,
        scratch_shapes=[
            pltpu.VMEM((T, dl), BF16),
            pltpu.VMEM((nch, dl, ch), BF16),
            pltpu.VMEM((T, ffl), F32),
            pltpu.VMEM((T, ffl), BF16),
            pltpu.VMEM((T, ffl), BF16),
            pltpu.VMEM((T, ffl), BF16),
            pltpu.VMEM((1, ffl), BF16),
            pltpu.VMEM((1, dl), BF16),
            pltpu.VMEM((nb, 8 * tps, ch), F32),
            pltpu.VMEM((nb, 8 * tps, ch), BF16),
            pltpu.VMEM((nb, 8 * tps, ch), BF16),
            pltpu.VMEM((nb, 4 * tps, ch), BF16),
            pltpu.VMEM((nb, 4 * tps, ch), BF16),
            pltpu.VMEM((nb, 4 * tps, ch), F32),
            pltpu.VMEM((nb, 3 * tps, ch), BF16),
            pltpu.VMEM((nb, 3 * tps, ch), BF16),
            pltpu.VMEM((nb, 2 * tps, ch), BF16),
            pltpu.VMEM((nb, tps, ch), BF16),
            dma((3,)),
            dma((nch,)),
            dma((nb,)),
            dma((32,)),
            dma((16,)),
            dma((4, nch)),
            dma((4, nch)),
            dma((2, nb)),
            dma((2, nb)),
            dma((2, nb)),
            dma((2, nb)),
            dma((3, nb)),
            dma((3, nb)),
            dma((2, nb)),
            dma((nb,)),
            pltpu.SemaphoreType.REGULAR,
        ],
        compiler_params=pltpu.CompilerParams(
            collective_id=0, has_side_effects=True, vmem_limit_bytes=63 * 1024 * 1024
        ),
    )(tokens, in_weight, in_bias.reshape(1, ffl), out_weight, out_bias.reshape(1, dl))


def solution(mesh):
    R, C, DP = mesh.shape["row"], mesh.shape["col"], mesh.shape["depth"]
    Y = C // CORES

    def body(tokens, in_weight, in_bias, out_weight, out_bias):
        if (R, C, DP) == (4, 2 * CORES, 2):
            return grid_call(tokens, in_weight, in_bias, out_weight, out_bias)
        tps, dl = tokens.shape
        ffl = in_weight.shape[1]
        T = tps * R * C
        ch = 512
        nch, nb = ffl // ch, dl // ch
        n_ag = 3 * R * Y + R
        vmem = pl.BlockSpec(memory_space=pltpu.VMEM)
        hbm = pl.BlockSpec(memory_space=pl.ANY)
        dma = pltpu.SemaphoreType.DMA
        return pl.pallas_call(
            functools.partial(general_kernel, R, C, DP, tps, nch, nb, ch),
            out_shape=jax.ShapeDtypeStruct((tps, dl), BF16),
            in_specs=[vmem, hbm, vmem, hbm, vmem],
            out_specs=vmem,
            scratch_shapes=[
                pltpu.VMEM((T, dl), BF16),
                pltpu.VMEM((nch, dl, ch), BF16),
                pltpu.VMEM((nch, T, ch), F32),
                pltpu.VMEM((nch, T, ch), BF16),
                pltpu.VMEM((DP - 1, nch, T, ch), BF16),
                pltpu.VMEM((T, ffl), BF16),
                pltpu.VMEM((nb, T, ch), F32),
                pltpu.VMEM((nb, T // CORES, ch), BF16),
                pltpu.VMEM((nb, T // CORES, ch), BF16),
                pltpu.VMEM((Y - 1, nb, R * tps, ch), BF16),
                pltpu.VMEM((Y - 1, nb, R * tps, ch), BF16),
                pltpu.VMEM((nb, R * tps, ch), F32),
                pltpu.VMEM((R - 1, nb, tps, ch), BF16),
                pltpu.VMEM((R - 1, nb, tps, ch), BF16),
                dma((nch,)),
                dma((nb,)),
                dma((n_ag,)),
                dma((R * C,)),
                dma((DP - 1, nch, 2)),
                dma((DP - 1, nch, 2)),
                dma((nb,)),
                dma((nb,)),
                dma((Y - 1, nb)),
                dma((Y - 1, nb)),
                dma((R - 1, nb)),
                dma((R - 1, nb)),
            ],
            compiler_params=pltpu.CompilerParams(
                collective_id=0, has_side_effects=True, vmem_limit_bytes=63 * 1024 * 1024
            ),
        )(tokens, in_weight, in_bias.reshape(1, ffl), out_weight, out_bias.reshape(1, dl))

    in_specs = (
        P(("row", "col"), "depth"),
        P("depth", ("row", "col")),
        P(("row", "col")),
        P(("row", "col"), "depth"),
        P("depth"),
    )
    out_specs = P(("row", "col"), "depth")
    return jax.shard_map(body, mesh=mesh, in_specs=in_specs, out_specs=out_specs, check_vma=False)
```

```python
import functools

import jax
import jax.numpy as jnp
from jax import lax
from jax.experimental import pallas as pl
from jax.experimental.pallas import tpu as pltpu
from jax.sharding import PartitionSpec as P

CORES = 2
BF16 = jnp.bfloat16
F32 = jnp.float32


def partner(i, step, n):
    if n & (n - 1):
        return (i + step) % n
    out, bit = 0, 1
    while bit < n:
        own = i // bit % 2
        out = out + bit * (1 - own if step & bit else own)
        bit *= 2
    return out


def general_kernel(
    R, C, DP, tps, nch, nb, ch,
    x_ref, w1_ref, b1_ref, w2_ref, b2_ref, out_ref,
    xbuf, slots, own, psend, precv, hbuf, acc, s1s, s1r, s2s, s2r, own2, s3s, s3r,
    w1_sem, w2_sem, ag_ss, ag_rs, p_ss, p_rs, s1_ss, s1_rs, s2_ss, s2_rs, s3_ss, s3_rs,
):
    Y = C // CORES
    z = lax.axis_index("row")
    col = lax.axis_index("col")
    dp = lax.axis_index("depth")
    y = col // CORES
    c = col % CORES
    sib = y * CORES + (1 - c)

    def remote(src, dst, ss, rs, **dev):
        return pltpu.make_async_remote_copy(
            src_ref=src, dst_ref=dst, send_sem=ss, recv_sem=rs,
            device_id=dev, device_id_type=pl.DeviceIdType.MESH,
        )

    def w1_copy(k):
        return pltpu.make_async_copy(w1_ref.at[:, pl.ds(pl.multiple_of(k * ch, ch), ch)], slots.at[k], w1_sem.at[k])

    ffl = w2_ref.shape[0]
    per = nb // nch

    def w2_slot(n):
        return n // per, pl.ds(pl.multiple_of(n % per * ffl, ffl), ffl)

    def w2_copy(n):
        return pltpu.make_async_copy(
            w2_ref.at[:, pl.ds(pl.multiple_of(n * ch, ch), ch)], slots.at[w2_slot(n)], w2_sem.at[n]
        )

    @pl.loop(0, nch)
    def _(k):
        w1_copy(k).start()

    barrier = pltpu.get_barrier_semaphore()

    def greet(**dev):
        pl.semaphore_signal(barrier, inc=1, device_id=dev, device_id_type=pl.DeviceIdType.MESH)

    z_peers = [partner(z, dz, R) for dz in range(1, R)]
    chain = R == 4
    far = 1 - z // (R // 2)
    if chain:
        z_order = [z, partner(z, 1, R), 1 + far, 3 * far]
        across = 3 - z
        inner = (z == 1) | (z == 2)
    else:
        z_order = [z] + z_peers
    y_peers = [(y + dy) % Y for dy in range(1, Y)]
    d_peers = [(dp + dd) % DP for dd in range(1, DP)]
    for zt in z_peers:
        greet(row=zt)
    for yt in y_peers:
        greet(col=yt * CORES + c)
    greet(col=sib)
    for dt in d_peers:
        greet(depth=dt)

    def shard(zz, yy, cc):
        return zz * C + yy * CORES + cc

    def rows(s):
        return pl.ds(pl.multiple_of(s * tps, tps), tps)

    me = shard(z, y, c)
    xbuf[rows(me)] = x_ref[...]
    pl.semaphore_wait(barrier, (R - 1) + (Y - 1) + 1 + (DP - 1))

    sent = []

    def send_shard(s, inner_only=False, **dev):
        copy = remote(xbuf.at[rows(s)], xbuf.at[rows(s)], ag_ss.at[len(sent)], ag_rs.at[s], **dev)
        sent.append((copy, inner_only))
        if inner_only:
            pl.when(inner)(copy.start)
        else:
            copy.start()

    def await_shard(s):
        remote(xbuf.at[rows(s)], xbuf.at[rows(s)], ag_ss.at[0], ag_rs.at[s], col=sib).wait_recv()

    if chain:
        send_shard(me, inner_only=True, row=across)
        send_shard(me, row=z_order[1])
    else:
        for zt in z_peers:
            send_shard(me, row=zt)
    for yt in y_peers:
        send_shard(me, col=yt * CORES + c)
    send_shard(me, col=sib)

    def forward_z(i):
        s = shard(z_order[i], y, c)
        await_shard(s)
        if chain:
            send_shard(s, inner_only=True, row=across if i == 1 else z_order[1])
        for yt in y_peers:
            send_shard(s, col=yt * CORES + c)
        send_shard(s, col=sib)

    def forward_y(i):
        for yt in y_peers:
            s = shard(z_order[i], yt, c)
            await_shard(s)
            send_shard(s, col=sib)

    half = R // 2

    def block_rows(b):
        size = half * C * tps
        return pl.ds(pl.multiple_of((1 - far if b == 0 else far) * size, size), size)

    def p_copy(i, k, b):
        r = block_rows(b)
        return remote(
            psend.at[k, r], precv.at[i, k, r], p_ss.at[i, k, b], p_rs.at[i, k, b], depth=d_peers[i]
        )

    def project(b, first, last):
        r = block_rows(b)

        @pl.loop(first, last)
        def _(k):
            if b == 0:
                w1_copy(k).wait()
            partial = jnp.dot(xbuf[r], slots[k], preferred_element_type=F32)
            own[k, r] = partial
            psend[k, r] = partial.astype(BF16)
            for i in range(DP - 1):
                p_copy(i, k, b).start()
            if b == 1:
                for j in range(per):
                    w2_copy(k * per + j).start()

    def await_block(b):
        for i in range(b * half, (b + 1) * half):
            for yt in [y] + y_peers:
                await_shard(shard(z_order[i], yt, 1 - c))

    for i in range(1, half):
        forward_z(i)
    for i in range(half):
        forward_y(i)
    forward_z(half)
    await_block(0)
    cut1, cut2 = nch // 3, 2 * nch // 3
    project(0, 0, cut1)
    for i in range(half + 1, R):
        forward_z(i)
    forward_y(half)
    project(0, cut1, cut2)
    for i in range(half + 1, R):
        forward_y(i)
    project(0, cut2, nch)
    await_block(1)
    project(1, 0, nch)

    def hidden(k):
        for i in range(DP - 1):
            for b in range(2):
                p_copy(i, k, b).wait_recv()
        pre = own[k]
        for i in range(DP - 1):
            pre = pre + precv[i, k].astype(F32)
        cols = pl.ds(pl.multiple_of(k * ch, ch), ch)
        pre = pre + b1_ref[:, cols].astype(F32)
        hbuf[:, cols] = jax.nn.gelu(pre, approximate=True).astype(BF16)

    def multiply(n):
        w2_copy(n).wait()
        acc[n] = jnp.dot(hbuf[...], slots[w2_slot(n)], preferred_element_type=F32)

    pl.loop(0, nch)(hidden)

    def s1_copy(n):
        return remote(s1s.at[n], s1r.at[n], s1_ss.at[n], s1_rs.at[n], col=sib)

    def s2_copy(i, n):
        return remote(s2s.at[i, n], s2r.at[i, n], s2_ss.at[i, n], s2_rs.at[i, n], col=y_peers[i] * CORES + c)

    def s3_copy(i, n):
        return remote(s3s.at[i, n], s3r.at[i, n], s3_ss.at[i, n], s3_rs.at[i, n], row=z_peers[i])

    def stage2(n):
        s1_copy(n).wait_recv()

        def chip_sum(j):
            return acc[n, rows(CORES * j + c)] + s1r[n, rows(j)].astype(F32)

        for i, yt in enumerate(y_peers):
            for zz in range(R):
                s2s[i, n, rows(zz)] = chip_sum(zz * Y + yt).astype(BF16)
            s2_copy(i, n).start()
        for zz in range(R):
            own2[n, rows(zz)] = chip_sum(zz * Y + y)

    @pl.loop(0, nb)
    def _(n):
        multiply(n)
        for j in range(R * Y):
            s1s[n, rows(j)] = acc[n, rows(CORES * j + 1 - c)].astype(BF16)
        s1_copy(n).start()

        @pl.when(n > 0)
        def _():
            stage2(n - 1)

    stage2(nb - 1)

    @pl.loop(0, nb)
    def _(n):
        total = own2[n]
        for i in range(Y - 1):
            s2_copy(i, n).wait_recv()
        for i in range(Y - 1):
            total = total + s2r[i, n].astype(F32)
        own2[n] = total
        for i, zt in enumerate(z_peers):
            s3s[i, n] = own2[n, rows(zt)].astype(BF16)
            s3_copy(i, n).start()

    @pl.loop(0, nb)
    def _(n):
        cols = pl.ds(pl.multiple_of(n * ch, ch), ch)
        for i in range(R - 1):
            s3_copy(i, n).wait_recv()
        total = own2[n, rows(z)]
        for i in range(R - 1):
            total = total + s3r[i, n].astype(F32)
        out_ref[:, cols] = (total + b2_ref[:, cols].astype(F32)).astype(BF16)

    for copy, inner_only in sent:
        if inner_only:
            pl.when(inner)(copy.wait_send)
        else:
            copy.wait_send()

    @pl.loop(0, nch)
    def _(k):
        for i in range(DP - 1):
            for b in range(2):
                p_copy(i, k, b).wait_send()

    @pl.loop(0, nb)
    def _(n):
        s1_copy(n).wait_send()
        for i in range(Y - 1):
            s2_copy(i, n).wait_send()
        for i in range(R - 1):
            s3_copy(i, n).wait_send()


def grid_kernel(
    tps, ch, lags,
    x_ref, w1_ref, b1_ref, w2_ref, b2_ref, out_ref,
    xbuf, slots, own, psend, precv, hbuf, b1l, b2l, b1v, b2v, s1s, s1r, s2s, s2r, own2, s3s, s3r, s4s, s4r,
    in_sem, w1_sem, w2_sem, ag_ss, ag_rs, p_ss, p_rs, s1_ss, s1_rs, s2_ss, s2_rs, s3_ss, s3_rs, s4_ss, s4_rs, far_sem,
):
    unit = CORES * tps
    ffl, dl = w2_ref.shape
    wide = 2 * ch
    nch, nw, nb = ffl // ch, ffl // wide, dl // wide
    z = lax.axis_index("row")
    col = lax.axis_index("col")
    dp = lax.axis_index("depth")
    y = col // CORES
    c = col % CORES
    inner = (z == 1) | (z == 2)
    end = jnp.logical_not(inner)
    SIB = {"col": y * CORES + (1 - c)}
    YN = {"col": (1 - y) * CORES + c}
    ZN = {"row": z + 1 - 2 * (z % 2)}
    ACROSS = {"row": 3 - z}
    FAR = {"row": 3 * (1 - z // 2)}
    XN = {"depth": 1 - dp}

    def remote(src, dst, ss, rs, dev):
        return pltpu.make_async_remote_copy(
            src_ref=src, dst_ref=dst, send_sem=ss, recv_sem=rs,
            device_id=dev, device_id_type=pl.DeviceIdType.MESH,
        )

    def signal(sem, dev):
        pl.semaphore_signal(sem, inc=1, device_id=dev, device_id_type=pl.DeviceIdType.MESH)

    barrier = pltpu.get_barrier_semaphore()
    for dev in (XN, YN, ZN, SIB):
        signal(barrier, dev)
    pl.when(inner)(lambda: signal(barrier, ACROSS))

    def span(k, size):
        return pl.ds(pl.multiple_of(k * size, size), size)

    x_copy = pltpu.make_async_copy(x_ref, xbuf.at[pl.ds(0, tps)], in_sem.at[0])
    b1_copy = pltpu.make_async_copy(b1_ref, b1l, in_sem.at[1])
    b2_copy = pltpu.make_async_copy(b2_ref, b2l, in_sem.at[2])
    x_copy.start()

    def w1_at(k):
        return span(k // 2, dl), span(k % 2, ch)

    def w1_copy(k):
        return pltpu.make_async_copy(w1_ref.at[:, span(k, ch)], slots.at[w1_at(k)], w1_sem.at[k])

    def w2_at(n):
        return span((n + nb) % (nb + 1), ffl)

    def w2_copy(n):
        return pltpu.make_async_copy(w2_ref.at[:, span(n, wide)], slots.at[w2_at(n)], w2_sem.at[n])

    @pl.loop(0, nch)
    def _(k):
        w1_copy(k).start()

    b1_copy.start()
    b2_copy.start()
    w2_copy(0).start()
    x_copy.wait()
    pl.semaphore_wait(barrier, 4 + (z % 3 + 1) // 2)

    def part(slot, rel, h):
        return pl.ds(slot * unit + rel * tps, tps), pl.ds(h * (dl // 2), dl // 2)

    sent = []

    def send(src, dst, h, dev, only=None):
        at = len(sent)

        def copy():
            return remote(xbuf.at[part(*src, h)], xbuf.at[part(*dst, h)], ag_ss.at[at], ag_rs.at[2 * dst[0] + dst[1], h], dev)

        sent.append((copy, only))
        if only is None:
            copy().start()
        else:
            pl.when(only)(lambda: copy().start())

    def landed(slot, rel, h):
        at = part(slot, rel, h)
        remote(xbuf.at[at], xbuf.at[at], ag_ss.at[0], ag_rs.at[2 * slot + rel, h], SIB).wait_recv()

    def landed_pair(*of):
        for slot in of:
            for h in range(2):
                landed(slot, 1, h)

    for h in range(2):
        send((0, 0), (0, 1), h, SIB)
        send((0, 0), (2, 0), h, ZN)
        send((0, 0), (3, 0), h, ACROSS, inner)
        send((0, 0), (1, 0), h, YN)
    pl.when(inner)(lambda: signal(far_sem, ACROSS))

    def first_hop(h):
        landed(2, 0, h)
        send((2, 0), (5, 0), h, ACROSS, inner)
        far_from_next(3, h, inner)
        if h == 0:
            send((2, 0), (7, 0), h, YN)
        send((2, 0), (2, 1), h, SIB)
        landed(1, 0, h)
        send((1, 0), (1, 1), h, SIB)

    def far_from_next(slot, h, only):
        pl.when(only)(lambda: landed(slot, 0, h))
        if only is inner:
            send((slot, 0), (slot, 0), h, ZN, only)
        send((slot, 0), (slot + 1, 0), h, YN, only)
        send((slot, 0), (slot, 1), h, SIB, only)

    def second_hop(h):
        far_from_next(5, h, inner)
        far_from_next(3, h, end)
        if h == 1:
            send((1, 0), (7, 0), h, ZN)

    def to_sibling(slot, h):
        landed(slot, 0, h)
        send((slot, 0), (slot, 1), h, SIB)

    def p_copy(kind, r0, nr, size, k):
        at = (pl.ds(r0, nr), span(k, size))
        return remote(psend.at[at], precv.at[at], p_ss.at[kind, k], p_rs.at[kind, k], XN)

    def keep(r0, k, value):
        nr = value.shape[0]
        own[k // 2, pl.ds(r0, nr), span(k % 2, ch)] = value
        psend[pl.ds(r0, nr), span(k, ch)] = value.astype(BF16)

    def project(block, k, pad=0):
        kind, r0, nr, size = block
        partial = jnp.dot(xbuf[pl.ds(r0 - pad, nr + pad)], slots[w1_at(k)], preferred_element_type=F32)
        keep(r0, k, partial[pad:])
        p_copy(*block, k).start()

    def hidden(r0, nr, k):
        at = (pl.ds(r0, nr), span(k, ch))
        pre = own[k // 2, pl.ds(r0, nr), span(k % 2, ch)] + precv[at].astype(F32) + b1v[k]
        hbuf[at] = jax.nn.gelu(pre, approximate=True).astype(BF16)

    early = 2 * nch // 3
    A = (0, 0, unit, ch)
    B = (1, unit, 2 * unit, ch)
    AB = (0, 0, 3 * unit, ch)
    C = (2, 3 * unit, 2 * unit, ch)
    D = (3, 5 * unit, 2 * unit, wide)
    E = (4, 7 * unit, unit, wide)

    for h in range(2):
        landed(0, 1, h)

    @pl.loop(0, early)
    def _(k):
        w1_copy(k).wait()
        pl.when(k == early - 1)(lambda: first_hop(0))
        project(A, k)

    first_hop(1)
    landed_pair(2, 1)

    @pl.loop(0, early)
    def _(k):
        pl.when(k == early // 2)(lambda: second_hop(0))
        project(B, k)

    second_hop(1)
    b1_copy.wait()
    b2_copy.wait()
    for k in range(nch):
        b1v[k] = b1l[pl.ds(k * ch, ch)].astype(F32).reshape(1, ch)
    for k in range(nb):
        b2v[k] = b2l[pl.ds(k * wide, wide)].astype(F32).reshape(1, wide)

    @pl.loop(early, nch)
    def _(k):
        w1_copy(k).wait()

        @pl.when(k == early + 1)
        def _():
            far_from_next(5, 0, end)
            to_sibling(4, 0)

        project(AB, k)

    to_sibling(4, 1)
    far_from_next(5, 1, end)
    landed_pair(3, 4)

    @pl.loop(0, nch)
    def _(k):
        project(C, k, 2 * unit)

    for slot in (7, 6):
        for h in range(2):
            to_sibling(slot, h)
    landed_pair(5, 7, 6)

    def first_arrived(k):
        @pl.when(k < early)
        def _():
            p_copy(*A, k).wait_recv()
            p_copy(*B, k).wait_recv()

        @pl.when(k >= early)
        def _():
            p_copy(*AB, k).wait_recv()

    @pl.loop(0, nw)
    def _(w):
        partial = jnp.dot(xbuf[pl.ds(4 * unit, 4 * unit)], slots[span(w, dl)], preferred_element_type=F32)
        for j in range(2):
            keep(5 * unit, 2 * w + j, partial[unit:, j * ch : (j + 1) * ch])
        p_copy(*D, w).start()
        for j in range(2):
            n = 2 * w + 1 + j
            pl.when(n < nb)(lambda n=n: w2_copy(n).start())
        for j in range(2):
            first_arrived(2 * w + j)
            hidden(0, 3 * unit, 2 * w + j)

    @pl.loop(0, nw)
    def _(w):
        p_copy(*E, w).start()

    @pl.loop(0, nch)
    def _(k):
        p_copy(*C, k).wait_recv()
        hidden(3 * unit, 2 * unit, k)

    PASSES = ((0, 5), (5, 2), (7, 1))
    KEPT = (((0, 0), (2, 1), (3, 2)), ((5, 3),), ())
    OVER_Y = (((1, 0), (4, 1)), ((6, 2),), ((7, 3),))
    FROM_Y = (0, 2, 3, 1)

    def sub(first, count=1):
        return pl.ds(first * tps, count * tps)

    def acc_at(p, n, j=0, count=1):
        first, total = PASSES[p]
        return n // 2, pl.ds(pl.multiple_of(first * unit + n % 2 * (total * tps) + j * tps, tps), count * tps)

    def s1_copy(p, n):
        at = (n, sub(*PASSES[p]))
        return remote(s1s.at[at], s1r.at[at], s1_ss.at[p, n], s1_rs.at[p, n], SIB)

    def s2_copy(p, n):
        at = (n, sub(OVER_Y[p][0][1], len(OVER_Y[p])))
        return remote(s2s.at[at], s2r.at[at], s2_ss.at[p, n], s2_rs.at[p, n], YN)

    def s3_copy(p, n):
        at = (n, sub(p))
        return remote(s3s.at[at], s3r.at[at], s3_ss.at[p, n], s3_rs.at[p, n], ZN)

    def s4_copy(p, n):
        return remote(s4s.at[n, sub(p)], s4r.at[n], s4_ss.at[p, n], s4_rs.at[n], FAR if p else ACROSS)

    def multiply(p, n):
        first, count = PASSES[p]
        pad = 0 if count > 4 else 4 - count
        if p == 0:
            w2_copy(n).wait()
        prod = jnp.dot(hbuf[pl.ds((first - pad) * unit, (count + pad) * unit)], slots[w2_at(n)], preferred_element_type=F32)
        for j in range(count):
            at = (j + pad) * unit
            own[acc_at(p, n, j)] = prod[at : at + tps]
            s1s[n, sub(first + j)] = prod[at + tps : at + unit].astype(BF16)
        s1_copy(p, n).start()

    def stage2(p, n):
        first, count = PASSES[p]
        s1_copy(p, n).wait_recv()

        def total(slot):
            return own[acc_at(p, n, slot - first)] + s1r[n, sub(slot)].astype(F32)

        for slot, to in OVER_Y[p]:
            s2s[n, sub(to)] = total(slot).astype(BF16)
        s2_copy(p, n).start()
        for slot, to in KEPT[p]:
            own2[n, sub(to)] = total(slot)

    def stage3(p, n):
        s2_copy(p, n).wait_recv()
        for slot, at in OVER_Y[p]:
            to = FROM_Y[at]
            total = own2[n, sub(to)] + s2r[n, sub(at)].astype(F32)
            if slot == 1:
                own2[n, sub(to)] = total
            elif slot == 7:
                s3s[n, sub(p)] = total.astype(BF16)
                s3_copy(p, n).start()
            else:
                @pl.when(end)
                def _():
                    s3s[n, sub(p)] = total.astype(BF16)
                    s3_copy(p, n).start()

                @pl.when(inner)
                def _():
                    own2[n, sub(to)] = total

    def stage4(p, n):
        if p < 2:
            @pl.when(inner)
            def _():
                s3_copy(p, n).wait_recv()
                total = own2[n, sub(2 + p)] + s3r[n, sub(p)].astype(F32)
                s4s[n, sub(p)] = total.astype(BF16)
                s4_copy(p, n).start()

    def finish(n):
        s4_copy(0, n).wait_recv()
        s3_copy(2, n).wait_recv()
        total = own2[n, sub(0)] + s3r[n, sub(2)].astype(F32) + s4r[n].astype(F32)
        out_ref[:, span(n, wide)] = (total + b2v[n]).astype(BF16)

    def stages(p, n):
        for stage, lag in zip((stage2, stage3, stage4), lags):
            for q in range(p + 1):
                m = n + (p - q) * nb - lag
                pl.when((m >= 0) & (m < nb))(lambda stage=stage, q=q, m=m: stage(q, m))

    @pl.loop(0, nb)
    def _(n):
        multiply(0, n)
        stages(0, n)

    @pl.loop(0, nw)
    def _(w):
        p_copy(*D, w).wait_recv()
        for j in range(2):
            hidden(5 * unit, 2 * unit, 2 * w + j)

    pl.when(inner)(lambda: pl.semaphore_wait(far_sem, 1))

    @pl.loop(0, nb)
    def _(n):
        multiply(1, n)
        stages(1, n)

    @pl.loop(0, nw)
    def _(w):
        p_copy(*E, w).wait_recv()
        for j in range(2):
            hidden(7 * unit, unit, 2 * w + j)

    @pl.loop(0, nb)
    def _(n):
        multiply(2, n)
        stages(2, n)

    @pl.loop(nb, nb + lags[2])
    def _(n):
        stages(2, n)

    pl.loop(0, nb)(finish)

    for copy, only in sent:
        if only is None:
            copy().wait_send()
        else:
            pl.when(only)(lambda copy=copy: copy().wait_send())

    @pl.loop(0, nch)
    def _(k):
        @pl.when(k < early)
        def _():
            p_copy(*A, k).wait_send()
            p_copy(*B, k).wait_send()

        @pl.when(k >= early)
        def _():
            p_copy(*AB, k).wait_send()

        p_copy(*C, k).wait_send()

    @pl.loop(0, nw)
    def _(w):
        p_copy(*D, w).wait_send()
        p_copy(*E, w).wait_send()

    @pl.loop(0, nb)
    def _(n):
        for p in range(3):
            s1_copy(p, n).wait_send()
            s2_copy(p, n).wait_send()
        s3_copy(2, n).wait_send()

        @pl.when(end)
        def _():
            s3_copy(0, n).wait_send()
            s3_copy(1, n).wait_send()

        @pl.when(inner)
        def _():
            s4_copy(0, n).wait_send()
            s4_copy(1, n).wait_send()


def grid_call(tokens, in_weight, in_bias, out_weight, out_bias):
    tps, dl = tokens.shape
    ffl = in_weight.shape[1]
    T = 16 * tps
    ch = 512
    wide = 2 * ch
    nch, nw, nb = ffl // ch, ffl // wide, dl // wide
    vmem = pl.BlockSpec(memory_space=pltpu.VMEM)
    hbm = pl.BlockSpec(memory_space=pl.ANY)
    dma = pltpu.SemaphoreType.DMA
    return pl.pallas_call(
        functools.partial(grid_kernel, tps, ch, (1, 4, 7)),
        out_shape=jax.ShapeDtypeStruct((tps, dl), BF16),
        in_specs=[hbm] * 5,
        out_specs=vmem,
        scratch_shapes=[
            pltpu.VMEM((T, dl), BF16),
            pltpu.VMEM(((nb + 1) * ffl, wide), BF16),
            pltpu.VMEM((nw, T, wide), F32),
            pltpu.VMEM((T, ffl), BF16),
            pltpu.VMEM((T, ffl), BF16),
            pltpu.VMEM((T, ffl), BF16),
            pltpu.VMEM((ffl,), BF16),
            pltpu.VMEM((dl,), BF16),
            pltpu.VMEM((nch, 1, ch), F32),
            pltpu.VMEM((nb, 1, wide), F32),
            pltpu.VMEM((nb, 8 * tps, wide), BF16),
            pltpu.VMEM((nb, 8 * tps, wide), BF16),
            pltpu.VMEM((nb, 4 * tps, wide), BF16),
            pltpu.VMEM((nb, 4 * tps, wide), BF16),
            pltpu.VMEM((nb, 4 * tps, wide), F32),
            pltpu.VMEM((nb, 3 * tps, wide), BF16),
            pltpu.VMEM((nb, 3 * tps, wide), BF16),
            pltpu.VMEM((nb, 2 * tps, wide), BF16),
            pltpu.VMEM((nb, tps, wide), BF16),
            dma((3,)),
            dma((nch,)),
            dma((nb,)),
            dma((48,)),
            dma((16, 2)),
            dma((5, nch)),
            dma((5, nch)),
            dma((3, nb)),
            dma((3, nb)),
            dma((3, nb)),
            dma((3, nb)),
            dma((3, nb)),
            dma((3, nb)),
            dma((2, nb)),
            dma((nb,)),
            pltpu.SemaphoreType.REGULAR,
        ],
        compiler_params=pltpu.CompilerParams(
            collective_id=0, has_side_effects=True, vmem_limit_bytes=63 * 1024 * 1024
        ),
    )(tokens, in_weight, in_bias, out_weight, out_bias)


def solution(mesh):
    R, C, DP = mesh.shape["row"], mesh.shape["col"], mesh.shape["depth"]
    Y = C // CORES

    def body(tokens, in_weight, in_bias, out_weight, out_bias):
        if (R, C, DP) == (4, 2 * CORES, 2):
            return grid_call(tokens, in_weight, in_bias, out_weight, out_bias)
        tps, dl = tokens.shape
        ffl = in_weight.shape[1]
        T = tps * R * C
        ch = 512
        nch, nb = ffl // ch, dl // ch
        n_ag = 3 * R * Y + R
        vmem = pl.BlockSpec(memory_space=pltpu.VMEM)
        hbm = pl.BlockSpec(memory_space=pl.ANY)
        dma = pltpu.SemaphoreType.DMA
        return pl.pallas_call(
            functools.partial(general_kernel, R, C, DP, tps, nch, nb, ch),
            out_shape=jax.ShapeDtypeStruct((tps, dl), BF16),
            in_specs=[vmem, hbm, vmem, hbm, vmem],
            out_specs=vmem,
            scratch_shapes=[
                pltpu.VMEM((T, dl), BF16),
                pltpu.VMEM((nch, dl, ch), BF16),
                pltpu.VMEM((nch, T, ch), F32),
                pltpu.VMEM((nch, T, ch), BF16),
                pltpu.VMEM((DP - 1, nch, T, ch), BF16),
                pltpu.VMEM((T, ffl), BF16),
                pltpu.VMEM((nb, T, ch), F32),
                pltpu.VMEM((nb, T // CORES, ch), BF16),
                pltpu.VMEM((nb, T // CORES, ch), BF16),
                pltpu.VMEM((Y - 1, nb, R * tps, ch), BF16),
                pltpu.VMEM((Y - 1, nb, R * tps, ch), BF16),
                pltpu.VMEM((nb, R * tps, ch), F32),
                pltpu.VMEM((R - 1, nb, tps, ch), BF16),
                pltpu.VMEM((R - 1, nb, tps, ch), BF16),
                dma((nch,)),
                dma((nb,)),
                dma((n_ag,)),
                dma((R * C,)),
                dma((DP - 1, nch, 2)),
                dma((DP - 1, nch, 2)),
                dma((nb,)),
                dma((nb,)),
                dma((Y - 1, nb)),
                dma((Y - 1, nb)),
                dma((R - 1, nb)),
                dma((R - 1, nb)),
            ],
            compiler_params=pltpu.CompilerParams(
                collective_id=0, has_side_effects=True, vmem_limit_bytes=63 * 1024 * 1024
            ),
        )(tokens, in_weight, in_bias.reshape(1, ffl), out_weight, out_bias.reshape(1, dl))

    in_specs = (
        P(("row", "col"), "depth"),
        P("depth", ("row", "col")),
        P(("row", "col")),
        P(("row", "col"), "depth"),
        P("depth"),
    )
    out_specs = P(("row", "col"), "depth")
    return jax.shard_map(body, mesh=mesh, in_specs=in_specs, out_specs=out_specs, check_vma=False)
```

```python
import functools

import jax
import jax.numpy as jnp
from jax import lax
from jax.experimental import pallas as pl
from jax.experimental.pallas import tpu as pltpu
from jax.sharding import PartitionSpec as P

CORES = 2
BF16 = jnp.bfloat16
F32 = jnp.float32


def partner(i, step, n):
    if n & (n - 1):
        return (i + step) % n
    out, bit = 0, 1
    while bit < n:
        own = i // bit % 2
        out = out + bit * (1 - own if step & bit else own)
        bit *= 2
    return out


def general_kernel(
    R, C, DP, tps, nch, nb, ch,
    x_ref, w1_ref, b1_ref, w2_ref, b2_ref, out_ref,
    xbuf, slots, own, psend, precv, hbuf, acc, s1s, s1r, s2s, s2r, own2, s3s, s3r,
    w1_sem, w2_sem, ag_ss, ag_rs, p_ss, p_rs, s1_ss, s1_rs, s2_ss, s2_rs, s3_ss, s3_rs,
):
    Y = C // CORES
    z = lax.axis_index("row")
    col = lax.axis_index("col")
    dp = lax.axis_index("depth")
    y = col // CORES
    c = col % CORES
    sib = y * CORES + (1 - c)

    def remote(src, dst, ss, rs, **dev):
        return pltpu.make_async_remote_copy(
            src_ref=src, dst_ref=dst, send_sem=ss, recv_sem=rs,
            device_id=dev, device_id_type=pl.DeviceIdType.MESH,
        )

    def w1_copy(k):
        return pltpu.make_async_copy(w1_ref.at[:, pl.ds(pl.multiple_of(k * ch, ch), ch)], slots.at[k], w1_sem.at[k])

    ffl = w2_ref.shape[0]
    per = nb // nch

    def w2_slot(n):
        return n // per, pl.ds(pl.multiple_of(n % per * ffl, ffl), ffl)

    def w2_copy(n):
        return pltpu.make_async_copy(
            w2_ref.at[:, pl.ds(pl.multiple_of(n * ch, ch), ch)], slots.at[w2_slot(n)], w2_sem.at[n]
        )

    @pl.loop(0, nch)
    def _(k):
        w1_copy(k).start()

    barrier = pltpu.get_barrier_semaphore()

    def greet(**dev):
        pl.semaphore_signal(barrier, inc=1, device_id=dev, device_id_type=pl.DeviceIdType.MESH)

    z_peers = [partner(z, dz, R) for dz in range(1, R)]
    chain = R == 4
    far = 1 - z // (R // 2)
    if chain:
        z_order = [z, partner(z, 1, R), 1 + far, 3 * far]
        across = 3 - z
        inner = (z == 1) | (z == 2)
    else:
        z_order = [z] + z_peers
    y_peers = [(y + dy) % Y for dy in range(1, Y)]
    d_peers = [(dp + dd) % DP for dd in range(1, DP)]
    for zt in z_peers:
        greet(row=zt)
    for yt in y_peers:
        greet(col=yt * CORES + c)
    greet(col=sib)
    for dt in d_peers:
        greet(depth=dt)

    def shard(zz, yy, cc):
        return zz * C + yy * CORES + cc

    def rows(s):
        return pl.ds(pl.multiple_of(s * tps, tps), tps)

    me = shard(z, y, c)
    xbuf[rows(me)] = x_ref[...]
    pl.semaphore_wait(barrier, (R - 1) + (Y - 1) + 1 + (DP - 1))

    sent = []

    def send_shard(s, inner_only=False, **dev):
        copy = remote(xbuf.at[rows(s)], xbuf.at[rows(s)], ag_ss.at[len(sent)], ag_rs.at[s], **dev)
        sent.append((copy, inner_only))
        if inner_only:
            pl.when(inner)(copy.start)
        else:
            copy.start()

    def await_shard(s):
        remote(xbuf.at[rows(s)], xbuf.at[rows(s)], ag_ss.at[0], ag_rs.at[s], col=sib).wait_recv()

    if chain:
        send_shard(me, inner_only=True, row=across)
        send_shard(me, row=z_order[1])
    else:
        for zt in z_peers:
            send_shard(me, row=zt)
    for yt in y_peers:
        send_shard(me, col=yt * CORES + c)
    send_shard(me, col=sib)

    def forward_z(i):
        s = shard(z_order[i], y, c)
        await_shard(s)
        if chain:
            send_shard(s, inner_only=True, row=across if i == 1 else z_order[1])
        for yt in y_peers:
            send_shard(s, col=yt * CORES + c)
        send_shard(s, col=sib)

    def forward_y(i):
        for yt in y_peers:
            s = shard(z_order[i], yt, c)
            await_shard(s)
            send_shard(s, col=sib)

    half = R // 2

    def block_rows(b):
        size = half * C * tps
        return pl.ds(pl.multiple_of((1 - far if b == 0 else far) * size, size), size)

    def p_copy(i, k, b):
        r = block_rows(b)
        return remote(
            psend.at[k, r], precv.at[i, k, r], p_ss.at[i, k, b], p_rs.at[i, k, b], depth=d_peers[i]
        )

    def project(b, first, last):
        r = block_rows(b)

        @pl.loop(first, last)
        def _(k):
            if b == 0:
                w1_copy(k).wait()
            partial = jnp.dot(xbuf[r], slots[k], preferred_element_type=F32)
            own[k, r] = partial
            psend[k, r] = partial.astype(BF16)
            for i in range(DP - 1):
                p_copy(i, k, b).start()
            if b == 1:
                for j in range(per):
                    w2_copy(k * per + j).start()

    def await_block(b):
        for i in range(b * half, (b + 1) * half):
            for yt in [y] + y_peers:
                await_shard(shard(z_order[i], yt, 1 - c))

    for i in range(1, half):
        forward_z(i)
    for i in range(half):
        forward_y(i)
    forward_z(half)
    await_block(0)
    cut1, cut2 = nch // 3, 2 * nch // 3
    project(0, 0, cut1)
    for i in range(half + 1, R):
        forward_z(i)
    forward_y(half)
    project(0, cut1, cut2)
    for i in range(half + 1, R):
        forward_y(i)
    project(0, cut2, nch)
    await_block(1)
    project(1, 0, nch)

    def hidden(k):
        for i in range(DP - 1):
            for b in range(2):
                p_copy(i, k, b).wait_recv()
        pre = own[k]
        for i in range(DP - 1):
            pre = pre + precv[i, k].astype(F32)
        cols = pl.ds(pl.multiple_of(k * ch, ch), ch)
        pre = pre + b1_ref[:, cols].astype(F32)
        hbuf[:, cols] = jax.nn.gelu(pre, approximate=True).astype(BF16)

    def multiply(n):
        w2_copy(n).wait()
        acc[n] = jnp.dot(hbuf[...], slots[w2_slot(n)], preferred_element_type=F32)

    pl.loop(0, nch)(hidden)

    def s1_copy(n):
        return remote(s1s.at[n], s1r.at[n], s1_ss.at[n], s1_rs.at[n], col=sib)

    def s2_copy(i, n):
        return remote(s2s.at[i, n], s2r.at[i, n], s2_ss.at[i, n], s2_rs.at[i, n], col=y_peers[i] * CORES + c)

    def s3_copy(i, n):
        return remote(s3s.at[i, n], s3r.at[i, n], s3_ss.at[i, n], s3_rs.at[i, n], row=z_peers[i])

    def stage2(n):
        s1_copy(n).wait_recv()

        def chip_sum(j):
            return acc[n, rows(CORES * j + c)] + s1r[n, rows(j)].astype(F32)

        for i, yt in enumerate(y_peers):
            for zz in range(R):
                s2s[i, n, rows(zz)] = chip_sum(zz * Y + yt).astype(BF16)
            s2_copy(i, n).start()
        for zz in range(R):
            own2[n, rows(zz)] = chip_sum(zz * Y + y)

    @pl.loop(0, nb)
    def _(n):
        multiply(n)
        for j in range(R * Y):
            s1s[n, rows(j)] = acc[n, rows(CORES * j + 1 - c)].astype(BF16)
        s1_copy(n).start()

        @pl.when(n > 0)
        def _():
            stage2(n - 1)

    stage2(nb - 1)

    @pl.loop(0, nb)
    def _(n):
        total = own2[n]
        for i in range(Y - 1):
            s2_copy(i, n).wait_recv()
        for i in range(Y - 1):
            total = total + s2r[i, n].astype(F32)
        own2[n] = total
        for i, zt in enumerate(z_peers):
            s3s[i, n] = own2[n, rows(zt)].astype(BF16)
            s3_copy(i, n).start()

    @pl.loop(0, nb)
    def _(n):
        cols = pl.ds(pl.multiple_of(n * ch, ch), ch)
        for i in range(R - 1):
            s3_copy(i, n).wait_recv()
        total = own2[n, rows(z)]
        for i in range(R - 1):
            total = total + s3r[i, n].astype(F32)
        out_ref[:, cols] = (total + b2_ref[:, cols].astype(F32)).astype(BF16)

    for copy, inner_only in sent:
        if inner_only:
            pl.when(inner)(copy.wait_send)
        else:
            copy.wait_send()

    @pl.loop(0, nch)
    def _(k):
        for i in range(DP - 1):
            for b in range(2):
                p_copy(i, k, b).wait_send()

    @pl.loop(0, nb)
    def _(n):
        s1_copy(n).wait_send()
        for i in range(Y - 1):
            s2_copy(i, n).wait_send()
        for i in range(R - 1):
            s3_copy(i, n).wait_send()


def grid_kernel(
    tps, ch, lags,
    x_ref, w1_ref, b1_ref, w2_ref, b2_ref, out_ref,
    xbuf, slots, own, psend, precv, b1l, b2l, b1v, b2v, s1r, s2r, s3r, s4s, s4r,
    in_sem, w1_sem, w2_sem, ag_ss, ag_rs, p_ss, p_rs, s1_ss, s1_rs, s2_ss, s2_rs, s3_ss, s3_rs, s4_ss, s4_rs, far_sem,
):
    unit = CORES * tps
    ffl, dl = w2_ref.shape
    wide = 2 * ch
    nch, nw, nb = ffl // ch, ffl // wide, dl // wide
    z = lax.axis_index("row")
    col = lax.axis_index("col")
    dp = lax.axis_index("depth")
    y = col // CORES
    c = col % CORES
    inner = (z == 1) | (z == 2)
    end = jnp.logical_not(inner)
    SIB = {"col": y * CORES + (1 - c)}
    YN = {"col": (1 - y) * CORES + c}
    ZN = {"row": z + 1 - 2 * (z % 2)}
    ACROSS = {"row": 3 - z}
    FAR = {"row": 3 * (1 - z // 2)}
    XN = {"depth": 1 - dp}

    def remote(src, dst, ss, rs, dev):
        return pltpu.make_async_remote_copy(
            src_ref=src, dst_ref=dst, send_sem=ss, recv_sem=rs,
            device_id=dev, device_id_type=pl.DeviceIdType.MESH,
        )

    def signal(sem, dev):
        pl.semaphore_signal(sem, inc=1, device_id=dev, device_id_type=pl.DeviceIdType.MESH)

    barrier = pltpu.get_barrier_semaphore()
    for dev in (XN, YN, ZN, SIB):
        signal(barrier, dev)
    pl.when(inner)(lambda: signal(barrier, ACROSS))

    def span(k, size):
        return pl.ds(pl.multiple_of(k * size, size), size)

    x_copy = pltpu.make_async_copy(x_ref, xbuf.at[pl.ds(0, tps)], in_sem.at[0])
    b1_copy = pltpu.make_async_copy(b1_ref, b1l, in_sem.at[1])
    b2_copy = pltpu.make_async_copy(b2_ref, b2l, in_sem.at[2])
    x_copy.start()

    def w1_at(k):
        return span(k // 2, dl), span(k % 2, ch)

    def w1_copy(k):
        return pltpu.make_async_copy(w1_ref.at[:, span(k, ch)], slots.at[w1_at(k)], w1_sem.at[k])

    def w2_at(n):
        return span((n + nb) % (nb + 2), ffl)

    def w2_copy(n):
        return pltpu.make_async_copy(w2_ref.at[:, span(n, wide)], slots.at[w2_at(n)], w2_sem.at[n])

    @pl.loop(0, nch)
    def _(k):
        w1_copy(k).start()

    b1_copy.start()
    b2_copy.start()
    for n in range(2):
        w2_copy(n).start()
    x_copy.wait()
    pl.semaphore_wait(barrier, 4 + (z % 3 + 1) // 2)

    def part(slot, rel, h):
        return pl.ds(slot * unit + rel * tps, tps), pl.ds(h * (dl // 2), dl // 2)

    sent = []

    def send(src, dst, h, dev, only=None):
        at = len(sent)

        def copy():
            return remote(xbuf.at[part(*src, h)], xbuf.at[part(*dst, h)], ag_ss.at[at], ag_rs.at[2 * dst[0] + dst[1], h], dev)

        sent.append((copy, only))
        if only is None:
            copy().start()
        else:
            pl.when(only)(lambda: copy().start())

    def landed(slot, rel, h):
        at = part(slot, rel, h)
        remote(xbuf.at[at], xbuf.at[at], ag_ss.at[0], ag_rs.at[2 * slot + rel, h], SIB).wait_recv()

    def landed_pair(*of):
        for slot in of:
            for h in range(2):
                landed(slot, 1, h)

    for h in range(2):
        send((0, 0), (0, 1), h, SIB)
        send((0, 0), (2, 0), h, ZN)
        send((0, 0), (3, 0), h, ACROSS, inner)
        send((0, 0), (1, 0), h, YN)
    pl.when(inner)(lambda: signal(far_sem, ACROSS))

    def first_hop(h):
        landed(2, 0, h)
        send((2, 0), (5, 0), h, ACROSS, inner)
        far_from_next(3, h, inner)
        if h == 0:
            send((2, 0), (7, 0), h, YN)
        send((2, 0), (2, 1), h, SIB)
        landed(1, 0, h)
        send((1, 0), (1, 1), h, SIB)

    def far_from_next(slot, h, only):
        pl.when(only)(lambda: landed(slot, 0, h))
        if only is inner:
            send((slot, 0), (slot, 0), h, ZN, only)
        send((slot, 0), (slot + 1, 0), h, YN, only)
        send((slot, 0), (slot, 1), h, SIB, only)

    def second_hop(h):
        far_from_next(5, h, inner)
        far_from_next(3, h, end)
        if h == 1:
            send((1, 0), (7, 0), h, ZN)

    def to_sibling(slot, h):
        landed(slot, 0, h)
        send((slot, 0), (slot, 1), h, SIB)

    def p_copy(kind, r0, nr, size, k):
        at = (pl.ds(r0, nr), span(k, size))
        return remote(psend.at[at], precv.at[at], p_ss.at[kind, k], p_rs.at[kind, k], XN)

    def keep(r0, k, value):
        nr = value.shape[0]
        own[k // 2, pl.ds(r0, nr), span(k % 2, ch)] = value
        psend[pl.ds(r0, nr), span(k, ch)] = value.astype(BF16)

    def project(block, k, pad=0):
        kind, r0, nr, size = block
        partial = jnp.dot(xbuf[pl.ds(r0 - pad, nr + pad)], slots[w1_at(k)], preferred_element_type=F32)
        keep(r0, k, partial[pad:])
        p_copy(*block, k).start()

    def hidden(r0, nr, k):
        at = (pl.ds(r0, nr), span(k, ch))
        pre = own[k // 2, pl.ds(r0, nr), span(k % 2, ch)] + precv[at].astype(F32) + b1v[k]
        precv[at] = jax.nn.gelu(pre, approximate=True).astype(BF16)

    early = 2 * nch // 3
    A = (0, 0, unit, ch)
    B = (1, unit, 2 * unit, ch)
    AB = (0, 0, 3 * unit, ch)
    C = (2, 3 * unit, 2 * unit, ch)
    D = (3, 5 * unit, 2 * unit, wide)
    E = (4, 7 * unit, unit, wide)

    for h in range(2):
        landed(0, 1, h)

    @pl.loop(0, early)
    def _(k):
        w1_copy(k).wait()
        pl.when(k == early - 1)(lambda: first_hop(0))
        project(A, k)

    first_hop(1)
    landed_pair(2, 1)

    @pl.loop(0, early)
    def _(k):
        pl.when(k == early // 2)(lambda: second_hop(0))
        project(B, k)

    second_hop(1)
    b1_copy.wait()
    b2_copy.wait()
    for k in range(nch):
        b1v[k] = b1l[pl.ds(k * ch, ch)].astype(F32).reshape(1, ch)
    for k in range(nb):
        b2v[k] = b2l[pl.ds(k * wide, wide)].astype(F32).reshape(1, wide)

    @pl.loop(early, nch)
    def _(k):
        w1_copy(k).wait()

        @pl.when(k == early + 1)
        def _():
            far_from_next(5, 0, end)
            to_sibling(4, 0)

        project(AB, k)

    to_sibling(4, 1)
    far_from_next(5, 1, end)
    landed_pair(3, 4)

    @pl.loop(0, nch)
    def _(k):
        @pl.when(k == 1)
        def _():
            to_sibling(7, 0)
            to_sibling(7, 1)

        pl.when(k == nch // 3)(lambda: to_sibling(6, 0))
        pl.when(k == 2 * nch // 3)(lambda: to_sibling(6, 1))
        project(C, k, 2 * unit)

    landed_pair(5, 7, 6)

    def first_arrived(k):
        @pl.when(k < early)
        def _():
            p_copy(*A, k).wait_recv()
            p_copy(*B, k).wait_recv()

        @pl.when(k >= early)
        def _():
            p_copy(*AB, k).wait_recv()

    @pl.loop(0, nw)
    def _(w):
        partial = jnp.dot(xbuf[pl.ds(4 * unit, 4 * unit)], slots[span(w, dl)], preferred_element_type=F32)
        for j in range(2):
            keep(5 * unit, 2 * w + j, partial[unit:, j * ch : (j + 1) * ch])
        p_copy(*D, w).start()
        for j in range(2):
            n = 2 * w + 2 + j
            pl.when(n < nb)(lambda n=n: w2_copy(n).start())
        for j in range(2):
            first_arrived(2 * w + j)
            hidden(0, 3 * unit, 2 * w + j)

    @pl.loop(0, nw)
    def _(w):
        p_copy(*E, w).start()

    @pl.loop(0, nch)
    def _(k):
        p_copy(*C, k).wait_recv()
        hidden(3 * unit, 2 * unit, k)

    for copy, only in sent:
        if only is None:
            copy().wait_send()
        else:
            pl.when(only)(lambda copy=copy: copy().wait_send())

    PASSES = ((0, 5), (5, 2), (7, 1))
    KEPT = ((0, 2, 3), (5,), ())
    OVER_Y = (1, 4, 6, 7)
    FROM_Y = (0, 3, 5, 2)

    def sub(first, count=1):
        return pl.ds(first * tps, count * tps)

    def acc_at(n, slot):
        first, total = PASSES[(slot >= PASSES[1][0]) + (slot >= PASSES[2][0])]
        return n // 2, pl.ds(pl.multiple_of(first * unit + n % 2 * (total * tps) + (slot - first) * tps, tps), tps)

    def s1_at(n, slot, count=1):
        return sub(slot, count), span(n, wide)

    def s2_at(n, i):
        return sub(8 + i), span(n, wide)

    def s3_at(n, i):
        return sub(12 + i), span(n, wide)

    def s1_copy(p, n):
        return remote(xbuf.at[s1_at(n, *PASSES[p])], s1r.at[n, sub(*PASSES[p])], s1_ss.at[p, n], s1_rs.at[p, n], SIB)

    def s2_copy(i, n):
        return remote(xbuf.at[s2_at(n, i)], s2r.at[n, sub(i)], s2_ss.at[i, n], s2_rs.at[i, n], YN)

    def s3_copy(i, n):
        return remote(xbuf.at[s3_at(n, i)], s3r.at[n, sub(i)], s3_ss.at[i, n], s3_rs.at[i, n], ZN)

    def s4_copy(p, n):
        return remote(s4s.at[n, sub(p)], s4r.at[n], s4_ss.at[p, n], s4_rs.at[n], FAR if p else ACROSS)

    def multiply(p, n):
        first, count = PASSES[p]
        pad = max(4 - count, 0)
        if p == 0:
            w2_copy(n).wait()
        prod = jnp.dot(precv[pl.ds((first - pad) * unit, (count + pad) * unit)], slots[w2_at(n)], preferred_element_type=F32)
        for j in range(count):
            at = (j + pad) * unit
            own[acc_at(n, first + j)] = prod[at : at + tps]
            xbuf[s1_at(n, first + j)] = prod[at + tps : at + unit].astype(BF16)
        s1_copy(p, n).start()

    def stage2(p, n):
        first, count = PASSES[p]
        s1_copy(p, n).wait_recv()

        def total(slot):
            return own[acc_at(n, slot)] + s1r[n, sub(slot)].astype(F32)

        for i, slot in enumerate(OVER_Y):
            if first <= slot < first + count:
                xbuf[s2_at(n, i)] = total(slot).astype(BF16)
                s2_copy(i, n).start()
        for slot in KEPT[p]:
            own[acc_at(n, slot)] = total(slot)

    def from_y(i, n):
        s2_copy(i, n).wait_recv()
        return own[acc_at(n, FROM_Y[i])] + s2r[n, sub(i)].astype(F32)

    def over_z(i, n, total):
        xbuf[s3_at(n, i)] = total.astype(BF16)
        s3_copy(i, n).start()

    def stage3(p, n):
        if p == 2:
            over_z(2, n, from_y(3, n))
            return
        if p == 0:
            own[acc_at(n, 0)] = from_y(0, n)
        i = 1 + p
        total = from_y(i, n)
        pl.when(end)(lambda: over_z(p, n, total))

        @pl.when(inner)
        def _():
            own[acc_at(n, FROM_Y[i])] = total

    def stage4(p, n):
        @pl.when(inner)
        def _():
            s3_copy(p, n).wait_recv()
            total = own[acc_at(n, FROM_Y[1 + p])] + s3r[n, sub(p)].astype(F32)
            s4s[n, sub(p)] = total.astype(BF16)
            s4_copy(p, n).start()

    def finish(n):
        s4_copy(0, n).wait_recv()
        s3_copy(2, n).wait_recv()
        total = own[acc_at(n, 0)] + s3r[n, sub(2)].astype(F32) + s4r[n].astype(F32)
        out_ref[:, span(n, wide)] = (total + b2v[n]).astype(BF16)

    def within(m, fn, *args):
        pl.when((m >= 0) & (m < nb))(lambda: fn(*args, m))

    def stages(p, n):
        for stage, lag in zip((stage2, stage3, stage4), lags):
            for q in range(min(p, 1) + 1 if stage is stage4 else p + 1):
                within(n + (p - q) * nb - lag, stage, q)

    @pl.loop(0, nb)
    def _(n):
        multiply(0, n)
        stages(0, n)

    @pl.loop(0, nw)
    def _(w):
        p_copy(*D, w).wait_recv()
        for j in range(2):
            hidden(5 * unit, 2 * unit, 2 * w + j)

    pl.when(inner)(lambda: pl.semaphore_wait(far_sem, 1))

    @pl.loop(0, nb)
    def _(n):
        multiply(1, n)
        stages(1, n)

    @pl.loop(0, nw)
    def _(w):
        p_copy(*E, w).wait_recv()
        for j in range(2):
            hidden(7 * unit, unit, 2 * w + j)

    @pl.loop(0, nb)
    def _(n):
        multiply(2, n)
        stages(2, n)

    @pl.loop(nb, nb + lags[2])
    def _(n):
        stages(2, n)

    pl.loop(0, nb)(finish)

    @pl.loop(0, nch)
    def _(k):
        @pl.when(k < early)
        def _():
            p_copy(*A, k).wait_send()
            p_copy(*B, k).wait_send()

        @pl.when(k >= early)
        def _():
            p_copy(*AB, k).wait_send()

        p_copy(*C, k).wait_send()

    @pl.loop(0, nw)
    def _(w):
        p_copy(*D, w).wait_send()
        p_copy(*E, w).wait_send()

    @pl.loop(0, nb)
    def _(n):
        for p in range(3):
            s1_copy(p, n).wait_send()
        for i in range(4):
            s2_copy(i, n).wait_send()
        s3_copy(2, n).wait_send()

        @pl.when(end)
        def _():
            s3_copy(0, n).wait_send()
            s3_copy(1, n).wait_send()

        @pl.when(inner)
        def _():
            s4_copy(0, n).wait_send()
            s4_copy(1, n).wait_send()


def grid_call(tokens, in_weight, in_bias, out_weight, out_bias):
    tps, dl = tokens.shape
    ffl = in_weight.shape[1]
    T = 16 * tps
    ch = 512
    wide = 2 * ch
    nch, nw, nb = ffl // ch, ffl // wide, dl // wide
    vmem = pl.BlockSpec(memory_space=pltpu.VMEM)
    hbm = pl.BlockSpec(memory_space=pl.ANY)
    dma = pltpu.SemaphoreType.DMA
    return pl.pallas_call(
        functools.partial(grid_kernel, tps, ch, (1, 4, 7)),
        out_shape=jax.ShapeDtypeStruct((tps, dl), BF16),
        in_specs=[hbm] * 5,
        out_specs=vmem,
        scratch_shapes=[
            pltpu.VMEM((T, dl), BF16),
            pltpu.VMEM(((nb + 2) * ffl, wide), BF16),
            pltpu.VMEM((nw, T, wide), F32),
            pltpu.VMEM((T, ffl), BF16),
            pltpu.VMEM((T, ffl), BF16),
            pltpu.VMEM((ffl,), BF16),
            pltpu.VMEM((dl,), BF16),
            pltpu.VMEM((nch, 1, ch), F32),
            pltpu.VMEM((nb, 1, wide), F32),
            pltpu.VMEM((nb, 8 * tps, wide), BF16),
            pltpu.VMEM((nb, 4 * tps, wide), BF16),
            pltpu.VMEM((nb, 3 * tps, wide), BF16),
            pltpu.VMEM((nb, 2 * tps, wide), BF16),
            pltpu.VMEM((nb, tps, wide), BF16),
            dma((3,)),
            dma((nch,)),
            dma((nb,)),
            dma((48,)),
            dma((16, 2)),
            dma((5, nch)),
            dma((5, nch)),
            dma((3, nb)),
            dma((3, nb)),
            dma((4, nb)),
            dma((4, nb)),
            dma((3, nb)),
            dma((3, nb)),
            dma((2, nb)),
            dma((nb,)),
            pltpu.SemaphoreType.REGULAR,
        ],
        compiler_params=pltpu.CompilerParams(
            collective_id=0, has_side_effects=True, vmem_limit_bytes=63 * 1024 * 1024
        ),
    )(tokens, in_weight, in_bias, out_weight, out_bias)


def solution(mesh):
    R, C, DP = mesh.shape["row"], mesh.shape["col"], mesh.shape["depth"]
    Y = C // CORES

    def body(tokens, in_weight, in_bias, out_weight, out_bias):
        if (R, C, DP) == (4, 2 * CORES, 2):
            return grid_call(tokens, in_weight, in_bias, out_weight, out_bias)
        tps, dl = tokens.shape
        ffl = in_weight.shape[1]
        T = tps * R * C
        ch = 512
        nch, nb = ffl // ch, dl // ch
        n_ag = 3 * R * Y + R
        vmem = pl.BlockSpec(memory_space=pltpu.VMEM)
        hbm = pl.BlockSpec(memory_space=pl.ANY)
        dma = pltpu.SemaphoreType.DMA
        return pl.pallas_call(
            functools.partial(general_kernel, R, C, DP, tps, nch, nb, ch),
            out_shape=jax.ShapeDtypeStruct((tps, dl), BF16),
            in_specs=[vmem, hbm, vmem, hbm, vmem],
            out_specs=vmem,
            scratch_shapes=[
                pltpu.VMEM((T, dl), BF16),
                pltpu.VMEM((nch, dl, ch), BF16),
                pltpu.VMEM((nch, T, ch), F32),
                pltpu.VMEM((nch, T, ch), BF16),
                pltpu.VMEM((DP - 1, nch, T, ch), BF16),
                pltpu.VMEM((T, ffl), BF16),
                pltpu.VMEM((nb, T, ch), F32),
                pltpu.VMEM((nb, T // CORES, ch), BF16),
                pltpu.VMEM((nb, T // CORES, ch), BF16),
                pltpu.VMEM((Y - 1, nb, R * tps, ch), BF16),
                pltpu.VMEM((Y - 1, nb, R * tps, ch), BF16),
                pltpu.VMEM((nb, R * tps, ch), F32),
                pltpu.VMEM((R - 1, nb, tps, ch), BF16),
                pltpu.VMEM((R - 1, nb, tps, ch), BF16),
                dma((nch,)),
                dma((nb,)),
                dma((n_ag,)),
                dma((R * C,)),
                dma((DP - 1, nch, 2)),
                dma((DP - 1, nch, 2)),
                dma((nb,)),
                dma((nb,)),
                dma((Y - 1, nb)),
                dma((Y - 1, nb)),
                dma((R - 1, nb)),
                dma((R - 1, nb)),
            ],
            compiler_params=pltpu.CompilerParams(
                collective_id=0, has_side_effects=True, vmem_limit_bytes=63 * 1024 * 1024
            ),
        )(tokens, in_weight, in_bias.reshape(1, ffl), out_weight, out_bias.reshape(1, dl))

    in_specs = (
        P(("row", "col"), "depth"),
        P("depth", ("row", "col")),
        P(("row", "col")),
        P(("row", "col"), "depth"),
        P("depth"),
    )
    out_specs = P(("row", "col"), "depth")
    return jax.shard_map(body, mesh=mesh, in_specs=in_specs, out_specs=out_specs, check_vma=False)
```

```python
import functools

import jax
import jax.numpy as jnp
from jax import lax
from jax.experimental import pallas as pl
from jax.experimental.pallas import tpu as pltpu
from jax.sharding import PartitionSpec as P

CORES = 2
BF16 = jnp.bfloat16
F32 = jnp.float32


def partner(i, step, n):
    if n & (n - 1):
        return (i + step) % n
    out, bit = 0, 1
    while bit < n:
        own = i // bit % 2
        out = out + bit * (1 - own if step & bit else own)
        bit *= 2
    return out


def general_kernel(
    R, C, DP, tps, nch, nb, ch,
    x_ref, w1_ref, b1_ref, w2_ref, b2_ref, out_ref,
    xbuf, slots, own, psend, precv, hbuf, acc, s1s, s1r, s2s, s2r, own2, s3s, s3r,
    w1_sem, w2_sem, ag_ss, ag_rs, p_ss, p_rs, s1_ss, s1_rs, s2_ss, s2_rs, s3_ss, s3_rs,
):
    Y = C // CORES
    z = lax.axis_index("row")
    col = lax.axis_index("col")
    dp = lax.axis_index("depth")
    y = col // CORES
    c = col % CORES
    sib = y * CORES + (1 - c)

    def remote(src, dst, ss, rs, **dev):
        return pltpu.make_async_remote_copy(
            src_ref=src, dst_ref=dst, send_sem=ss, recv_sem=rs,
            device_id=dev, device_id_type=pl.DeviceIdType.MESH,
        )

    def w1_copy(k):
        return pltpu.make_async_copy(w1_ref.at[:, pl.ds(pl.multiple_of(k * ch, ch), ch)], slots.at[k], w1_sem.at[k])

    ffl = w2_ref.shape[0]
    per = nb // nch

    def w2_slot(n):
        return n // per, pl.ds(pl.multiple_of(n % per * ffl, ffl), ffl)

    def w2_copy(n):
        return pltpu.make_async_copy(
            w2_ref.at[:, pl.ds(pl.multiple_of(n * ch, ch), ch)], slots.at[w2_slot(n)], w2_sem.at[n]
        )

    @pl.loop(0, nch)
    def _(k):
        w1_copy(k).start()

    barrier = pltpu.get_barrier_semaphore()

    def greet(**dev):
        pl.semaphore_signal(barrier, inc=1, device_id=dev, device_id_type=pl.DeviceIdType.MESH)

    z_peers = [partner(z, dz, R) for dz in range(1, R)]
    chain = R == 4
    far = 1 - z // (R // 2)
    if chain:
        z_order = [z, partner(z, 1, R), 1 + far, 3 * far]
        across = 3 - z
        inner = (z == 1) | (z == 2)
    else:
        z_order = [z] + z_peers
    y_peers = [(y + dy) % Y for dy in range(1, Y)]
    d_peers = [(dp + dd) % DP for dd in range(1, DP)]
    for zt in z_peers:
        greet(row=zt)
    for yt in y_peers:
        greet(col=yt * CORES + c)
    greet(col=sib)
    for dt in d_peers:
        greet(depth=dt)

    def shard(zz, yy, cc):
        return zz * C + yy * CORES + cc

    def rows(s):
        return pl.ds(pl.multiple_of(s * tps, tps), tps)

    me = shard(z, y, c)
    xbuf[rows(me)] = x_ref[...]
    pl.semaphore_wait(barrier, (R - 1) + (Y - 1) + 1 + (DP - 1))

    sent = []

    def send_shard(s, inner_only=False, **dev):
        copy = remote(xbuf.at[rows(s)], xbuf.at[rows(s)], ag_ss.at[len(sent)], ag_rs.at[s], **dev)
        sent.append((copy, inner_only))
        if inner_only:
            pl.when(inner)(copy.start)
        else:
            copy.start()

    def await_shard(s):
        remote(xbuf.at[rows(s)], xbuf.at[rows(s)], ag_ss.at[0], ag_rs.at[s], col=sib).wait_recv()

    if chain:
        send_shard(me, inner_only=True, row=across)
        send_shard(me, row=z_order[1])
    else:
        for zt in z_peers:
            send_shard(me, row=zt)
    for yt in y_peers:
        send_shard(me, col=yt * CORES + c)
    send_shard(me, col=sib)

    def forward_z(i):
        s = shard(z_order[i], y, c)
        await_shard(s)
        if chain:
            send_shard(s, inner_only=True, row=across if i == 1 else z_order[1])
        for yt in y_peers:
            send_shard(s, col=yt * CORES + c)
        send_shard(s, col=sib)

    def forward_y(i):
        for yt in y_peers:
            s = shard(z_order[i], yt, c)
            await_shard(s)
            send_shard(s, col=sib)

    half = R // 2

    def block_rows(b):
        size = half * C * tps
        return pl.ds(pl.multiple_of((1 - far if b == 0 else far) * size, size), size)

    def p_copy(i, k, b):
        r = block_rows(b)
        return remote(
            psend.at[k, r], precv.at[i, k, r], p_ss.at[i, k, b], p_rs.at[i, k, b], depth=d_peers[i]
        )

    def project(b, first, last):
        r = block_rows(b)

        @pl.loop(first, last)
        def _(k):
            if b == 0:
                w1_copy(k).wait()
            partial = jnp.dot(xbuf[r], slots[k], preferred_element_type=F32)
            own[k, r] = partial
            psend[k, r] = partial.astype(BF16)
            for i in range(DP - 1):
                p_copy(i, k, b).start()
            if b == 1:
                for j in range(per):
                    w2_copy(k * per + j).start()

    def await_block(b):
        for i in range(b * half, (b + 1) * half):
            for yt in [y] + y_peers:
                await_shard(shard(z_order[i], yt, 1 - c))

    for i in range(1, half):
        forward_z(i)
    for i in range(half):
        forward_y(i)
    forward_z(half)
    await_block(0)
    cut1, cut2 = nch // 3, 2 * nch // 3
    project(0, 0, cut1)
    for i in range(half + 1, R):
        forward_z(i)
    forward_y(half)
    project(0, cut1, cut2)
    for i in range(half + 1, R):
        forward_y(i)
    project(0, cut2, nch)
    await_block(1)
    project(1, 0, nch)

    def hidden(k):
        for i in range(DP - 1):
            for b in range(2):
                p_copy(i, k, b).wait_recv()
        pre = own[k]
        for i in range(DP - 1):
            pre = pre + precv[i, k].astype(F32)
        cols = pl.ds(pl.multiple_of(k * ch, ch), ch)
        pre = pre + b1_ref[:, cols].astype(F32)
        hbuf[:, cols] = jax.nn.gelu(pre, approximate=True).astype(BF16)

    def multiply(n):
        w2_copy(n).wait()
        acc[n] = jnp.dot(hbuf[...], slots[w2_slot(n)], preferred_element_type=F32)

    pl.loop(0, nch)(hidden)

    def s1_copy(n):
        return remote(s1s.at[n], s1r.at[n], s1_ss.at[n], s1_rs.at[n], col=sib)

    def s2_copy(i, n):
        return remote(s2s.at[i, n], s2r.at[i, n], s2_ss.at[i, n], s2_rs.at[i, n], col=y_peers[i] * CORES + c)

    def s3_copy(i, n):
        return remote(s3s.at[i, n], s3r.at[i, n], s3_ss.at[i, n], s3_rs.at[i, n], row=z_peers[i])

    def stage2(n):
        s1_copy(n).wait_recv()

        def chip_sum(j):
            return acc[n, rows(CORES * j + c)] + s1r[n, rows(j)].astype(F32)

        for i, yt in enumerate(y_peers):
            for zz in range(R):
                s2s[i, n, rows(zz)] = chip_sum(zz * Y + yt).astype(BF16)
            s2_copy(i, n).start()
        for zz in range(R):
            own2[n, rows(zz)] = chip_sum(zz * Y + y)

    @pl.loop(0, nb)
    def _(n):
        multiply(n)
        for j in range(R * Y):
            s1s[n, rows(j)] = acc[n, rows(CORES * j + 1 - c)].astype(BF16)
        s1_copy(n).start()

        @pl.when(n > 0)
        def _():
            stage2(n - 1)

    stage2(nb - 1)

    @pl.loop(0, nb)
    def _(n):
        total = own2[n]
        for i in range(Y - 1):
            s2_copy(i, n).wait_recv()
        for i in range(Y - 1):
            total = total + s2r[i, n].astype(F32)
        own2[n] = total
        for i, zt in enumerate(z_peers):
            s3s[i, n] = own2[n, rows(zt)].astype(BF16)
            s3_copy(i, n).start()

    @pl.loop(0, nb)
    def _(n):
        cols = pl.ds(pl.multiple_of(n * ch, ch), ch)
        for i in range(R - 1):
            s3_copy(i, n).wait_recv()
        total = own2[n, rows(z)]
        for i in range(R - 1):
            total = total + s3r[i, n].astype(F32)
        out_ref[:, cols] = (total + b2_ref[:, cols].astype(F32)).astype(BF16)

    for copy, inner_only in sent:
        if inner_only:
            pl.when(inner)(copy.wait_send)
        else:
            copy.wait_send()

    @pl.loop(0, nch)
    def _(k):
        for i in range(DP - 1):
            for b in range(2):
                p_copy(i, k, b).wait_send()

    @pl.loop(0, nb)
    def _(n):
        s1_copy(n).wait_send()
        for i in range(Y - 1):
            s2_copy(i, n).wait_send()
        for i in range(R - 1):
            s3_copy(i, n).wait_send()


def grid_kernel(
    tps, ch, lags,
    x_ref, w1_ref, b1_ref, w2_ref, b2_ref, out_ref,
    xbuf, slots, own, psend, precv, b1l, b2l, b1v, b2v, s1r, s2r, s3r, s4s, s4r,
    in_sem, w1_sem, w2_sem, ag_ss, ag_rs, p_ss, p_rs, s1_ss, s1_rs, s2_ss, s2_rs, s3_ss, s3_rs, s4_ss, s4_rs, far_sem,
):
    unit = CORES * tps
    ffl, dl = w2_ref.shape
    wide = 2 * ch
    nch, nw, nb = ffl // ch, ffl // wide, dl // wide
    z = lax.axis_index("row")
    col = lax.axis_index("col")
    dp = lax.axis_index("depth")
    y = col // CORES
    c = col % CORES
    inner = (z == 1) | (z == 2)
    end = jnp.logical_not(inner)
    SIB = {"col": y * CORES + (1 - c)}
    YN = {"col": (1 - y) * CORES + c}
    ZN = {"row": z + 1 - 2 * (z % 2)}
    ACROSS = {"row": 3 - z}
    FAR = {"row": 3 * (1 - z // 2)}
    XN = {"depth": 1 - dp}

    def remote(src, dst, ss, rs, dev):
        return pltpu.make_async_remote_copy(
            src_ref=src, dst_ref=dst, send_sem=ss, recv_sem=rs,
            device_id=dev, device_id_type=pl.DeviceIdType.MESH,
        )

    def signal(sem, dev):
        pl.semaphore_signal(sem, inc=1, device_id=dev, device_id_type=pl.DeviceIdType.MESH)

    barrier = pltpu.get_barrier_semaphore()
    for dev in (XN, YN, ZN, SIB):
        signal(barrier, dev)
    pl.when(inner)(lambda: signal(barrier, ACROSS))

    def span(k, size):
        return pl.ds(pl.multiple_of(k * size, size), size)

    x_copy = pltpu.make_async_copy(x_ref, xbuf.at[pl.ds(0, tps)], in_sem.at[0])
    b1_copy = pltpu.make_async_copy(b1_ref, b1l, in_sem.at[1])
    b2_copy = pltpu.make_async_copy(b2_ref, b2l, in_sem.at[2])
    x_copy.start()

    def w1_at(k):
        return span(k // 2, dl), span(k % 2, ch)

    def w1_copy(k):
        return pltpu.make_async_copy(w1_ref.at[:, span(k, ch)], slots.at[w1_at(k)], w1_sem.at[k])

    def w2_at(n):
        return span((n + nb) % (nb + 2), ffl)

    def w2_copy(n):
        return pltpu.make_async_copy(w2_ref.at[:, span(n, wide)], slots.at[w2_at(n)], w2_sem.at[n])

    @pl.loop(0, nch)
    def _(k):
        w1_copy(k).start()

    b1_copy.start()
    b2_copy.start()
    for n in range(2):
        w2_copy(n).start()
    x_copy.wait()
    pl.semaphore_wait(barrier, 4 + (z % 3 + 1) // 2)

    def part(slot, rel, h):
        return pl.ds(slot * unit + rel * tps, tps), pl.ds(h * (dl // 2), dl // 2)

    sent = []

    def send(src, dst, h, dev, only=None):
        at = len(sent)

        def copy():
            return remote(xbuf.at[part(*src, h)], xbuf.at[part(*dst, h)], ag_ss.at[at], ag_rs.at[2 * dst[0] + dst[1], h], dev)

        sent.append((copy, only))
        if only is None:
            copy().start()
        else:
            pl.when(only)(lambda: copy().start())

    def landed(slot, rel, h):
        at = part(slot, rel, h)
        remote(xbuf.at[at], xbuf.at[at], ag_ss.at[0], ag_rs.at[2 * slot + rel, h], SIB).wait_recv()

    def landed_pair(*of):
        for slot in of:
            for h in range(2):
                landed(slot, 1, h)

    for h in range(2):
        send((0, 0), (0, 1), h, SIB)
        send((0, 0), (2, 0), h, ZN)
        send((0, 0), (3, 0), h, ACROSS, inner)
        send((0, 0), (1, 0), h, YN)
    pl.when(inner)(lambda: signal(far_sem, ACROSS))

    def first_hop(h):
        landed(2, 0, h)
        send((2, 0), (5, 0), h, ACROSS, inner)
        far_from_next(3, h, inner)
        if h == 0:
            send((2, 0), (7, 0), h, YN)
        send((2, 0), (2, 1), h, SIB)
        landed(1, 0, h)
        send((1, 0), (1, 1), h, SIB)

    def far_from_next(slot, h, only):
        pl.when(only)(lambda: landed(slot, 0, h))
        if only is inner:
            send((slot, 0), (slot, 0), h, ZN, only)
        send((slot, 0), (slot + 1, 0), h, YN, only)
        send((slot, 0), (slot, 1), h, SIB, only)

    def second_hop(h):
        far_from_next(5, h, inner)
        far_from_next(3, h, end)
        if h == 1:
            send((1, 0), (7, 0), h, ZN)

    def to_sibling(slot, h):
        landed(slot, 0, h)
        send((slot, 0), (slot, 1), h, SIB)

    def p_copy(kind, r0, nr, size, k):
        at = (pl.ds(r0, nr), span(k, size))
        return remote(psend.at[at], precv.at[at], p_ss.at[kind, k], p_rs.at[kind, k], XN)

    def keep(r0, k, value):
        nr = value.shape[0]
        own[k // 2, pl.ds(r0, nr), span(k % 2, ch)] = value
        psend[pl.ds(r0, nr), span(k, ch)] = value.astype(BF16)

    def project(block, k, pad=0):
        kind, r0, nr, size = block
        partial = jnp.dot(xbuf[pl.ds(r0 - pad, nr + pad)], slots[w1_at(k)], preferred_element_type=F32)
        keep(r0, k, partial[pad:])
        p_copy(*block, k).start()

    def hidden(r0, nr, k):
        at = (pl.ds(r0, nr), span(k, ch))
        pre = own[k // 2, pl.ds(r0, nr), span(k % 2, ch)] + precv[at].astype(F32) + b1v[k]
        precv[at] = jax.nn.gelu(pre, approximate=True).astype(BF16)

    early = 2 * nch // 3
    A = (0, 0, unit, ch)
    B = (1, unit, 2 * unit, ch)
    AB = (0, 0, 3 * unit, ch)
    C = (2, 3 * unit, 2 * unit, ch)
    D = (3, 5 * unit, 2 * unit, wide)
    E = (4, 7 * unit, unit, wide)

    for h in range(2):
        landed(0, 1, h)

    @pl.loop(0, early)
    def _(k):
        w1_copy(k).wait()
        pl.when(k == early - 1)(lambda: first_hop(0))
        project(A, k)

    first_hop(1)
    landed_pair(2, 1)

    @pl.loop(0, early)
    def _(k):
        pl.when(k == early // 2)(lambda: second_hop(0))
        project(B, k)

    second_hop(1)
    b1_copy.wait()
    b2_copy.wait()
    for k in range(nch):
        b1v[k] = b1l[pl.ds(k * ch, ch)].astype(F32).reshape(1, ch)
    for k in range(nb):
        b2v[k] = b2l[pl.ds(k * wide, wide)].astype(F32).reshape(1, wide)

    @pl.loop(early, nch)
    def _(k):
        w1_copy(k).wait()

        @pl.when(k == early + 1)
        def _():
            far_from_next(5, 0, end)
            to_sibling(4, 0)

        project(AB, k)

    to_sibling(4, 1)
    far_from_next(5, 1, end)

    @pl.loop(0, early)
    def _(k):
        p_copy(*A, k).wait_recv()
        p_copy(*B, k).wait_recv()
        hidden(0, 3 * unit, k)

    landed_pair(3, 4)

    @pl.loop(0, nch)
    def _(k):
        @pl.when(k == 1)
        def _():
            to_sibling(7, 0)
            to_sibling(7, 1)

        pl.when(k == nch // 3)(lambda: to_sibling(6, 0))
        pl.when(k == 2 * nch // 3)(lambda: to_sibling(6, 1))
        project(C, k, 2 * unit)

    landed_pair(5, 7, 6)

    @pl.loop(0, nw)
    def _(w):
        partial = jnp.dot(xbuf[pl.ds(4 * unit, 4 * unit)], slots[span(w, dl)], preferred_element_type=F32)
        for j in range(2):
            keep(5 * unit, 2 * w + j, partial[unit:, j * ch : (j + 1) * ch])
        p_copy(*D, w).start()
        for j in range(2):
            n = 2 * w + 2 + j
            pl.when(n < nb)(lambda n=n: w2_copy(n).start())
        for j in range(2):
            k = 2 * w + j

            @pl.when(k >= early)
            def _(k=k):
                p_copy(*AB, k).wait_recv()
                hidden(0, 3 * unit, k)

    @pl.loop(0, nw)
    def _(w):
        p_copy(*E, w).start()

    @pl.loop(0, nch)
    def _(k):
        p_copy(*C, k).wait_recv()
        hidden(3 * unit, 2 * unit, k)

    for copy, only in sent:
        if only is None:
            copy().wait_send()
        else:
            pl.when(only)(lambda copy=copy: copy().wait_send())

    PASSES = ((0, 5), (5, 2), (7, 1))
    KEPT = ((0, 2, 3), (5,), ())
    OVER_Y = (1, 4, 6, 7)
    FROM_Y = (0, 3, 5, 2)

    def sub(first, count=1):
        return pl.ds(first * tps, count * tps)

    def acc_at(n, slot):
        first, total = PASSES[(slot >= PASSES[1][0]) + (slot >= PASSES[2][0])]
        return n // 2, pl.ds(pl.multiple_of(first * unit + n % 2 * (total * tps) + (slot - first) * tps, tps), tps)

    def s1_at(n, slot, count=1):
        return sub(slot, count), span(n, wide)

    def s2_at(n, i):
        return sub(8 + i), span(n, wide)

    def s3_at(n, i):
        return sub(12 + i), span(n, wide)

    def s1_copy(p, n):
        return remote(xbuf.at[s1_at(n, *PASSES[p])], s1r.at[n, sub(*PASSES[p])], s1_ss.at[p, n], s1_rs.at[p, n], SIB)

    def s2_copy(i, n):
        return remote(xbuf.at[s2_at(n, i)], s2r.at[n, sub(i)], s2_ss.at[i, n], s2_rs.at[i, n], YN)

    def s3_copy(i, n):
        return remote(xbuf.at[s3_at(n, i)], s3r.at[n, sub(i)], s3_ss.at[i, n], s3_rs.at[i, n], ZN)

    def s4_copy(p, n):
        return remote(s4s.at[n, sub(p)], s4r.at[n], s4_ss.at[p, n], s4_rs.at[n], FAR if p else ACROSS)

    def multiply(p, n):
        first, count = PASSES[p]
        pad = max(4 - count, 0)
        if p == 0:
            w2_copy(n).wait()
        prod = jnp.dot(precv[pl.ds((first - pad) * unit, (count + pad) * unit)], slots[w2_at(n)], preferred_element_type=F32)
        for j in range(count):
            at = (j + pad) * unit
            own[acc_at(n, first + j)] = prod[at : at + tps]
            xbuf[s1_at(n, first + j)] = prod[at + tps : at + unit].astype(BF16)
        s1_copy(p, n).start()

    def stage2(p, n):
        first, count = PASSES[p]
        s1_copy(p, n).wait_recv()

        def total(slot):
            return own[acc_at(n, slot)] + s1r[n, sub(slot)].astype(F32)

        for i, slot in enumerate(OVER_Y):
            if first <= slot < first + count:
                xbuf[s2_at(n, i)] = total(slot).astype(BF16)
                s2_copy(i, n).start()
        for slot in KEPT[p]:
            own[acc_at(n, slot)] = total(slot)

    def from_y(i, n):
        s2_copy(i, n).wait_recv()
        return own[acc_at(n, FROM_Y[i])] + s2r[n, sub(i)].astype(F32)

    def over_z(i, n, total):
        xbuf[s3_at(n, i)] = total.astype(BF16)
        s3_copy(i, n).start()

    def stage3(p, n):
        if p == 2:
            over_z(2, n, from_y(3, n))
            return
        if p == 0:
            own[acc_at(n, 0)] = from_y(0, n)
        i = 1 + p
        total = from_y(i, n)
        pl.when(end)(lambda: over_z(p, n, total))

        @pl.when(inner)
        def _():
            own[acc_at(n, FROM_Y[i])] = total

    def stage4(p, n):
        @pl.when(inner)
        def _():
            s3_copy(p, n).wait_recv()
            total = own[acc_at(n, FROM_Y[1 + p])] + s3r[n, sub(p)].astype(F32)
            s4s[n, sub(p)] = total.astype(BF16)
            s4_copy(p, n).start()

    def finish(n):
        s4_copy(0, n).wait_recv()
        s3_copy(2, n).wait_recv()
        total = own[acc_at(n, 0)] + s3r[n, sub(2)].astype(F32) + s4r[n].astype(F32)
        out_ref[:, span(n, wide)] = (total + b2v[n]).astype(BF16)

    def within(m, fn, *args):
        pl.when((m >= 0) & (m < nb))(lambda: fn(*args, m))

    def stages(p, n):
        for stage, lag in zip((stage2, stage3, stage4), lags):
            for q in range(min(p, 1) + 1 if stage is stage4 else p + 1):
                within(n + (p - q) * nb - lag, stage, q)

    @pl.loop(0, nb)
    def _(n):
        multiply(0, n)
        stages(0, n)

    @pl.loop(0, nw)
    def _(w):
        p_copy(*D, w).wait_recv()
        for j in range(2):
            hidden(5 * unit, 2 * unit, 2 * w + j)

    pl.when(inner)(lambda: pl.semaphore_wait(far_sem, 1))

    @pl.loop(0, nb)
    def _(n):
        multiply(1, n)
        stages(1, n)

    @pl.loop(0, nw)
    def _(w):
        p_copy(*E, w).wait_recv()
        for j in range(2):
            hidden(7 * unit, unit, 2 * w + j)

    @pl.loop(0, nb)
    def _(n):
        multiply(2, n)
        stages(2, n)

    @pl.loop(nb, nb + lags[2])
    def _(n):
        stages(2, n)

    pl.loop(0, nb)(finish)

    @pl.loop(0, nch)
    def _(k):
        @pl.when(k < early)
        def _():
            p_copy(*A, k).wait_send()
            p_copy(*B, k).wait_send()

        @pl.when(k >= early)
        def _():
            p_copy(*AB, k).wait_send()

        p_copy(*C, k).wait_send()

    @pl.loop(0, nw)
    def _(w):
        p_copy(*D, w).wait_send()
        p_copy(*E, w).wait_send()

    @pl.loop(0, nb)
    def _(n):
        for p in range(3):
            s1_copy(p, n).wait_send()
        for i in range(4):
            s2_copy(i, n).wait_send()
        s3_copy(2, n).wait_send()

        @pl.when(end)
        def _():
            s3_copy(0, n).wait_send()
            s3_copy(1, n).wait_send()

        @pl.when(inner)
        def _():
            s4_copy(0, n).wait_send()
            s4_copy(1, n).wait_send()


def grid_call(tokens, in_weight, in_bias, out_weight, out_bias):
    tps, dl = tokens.shape
    ffl = in_weight.shape[1]
    T = 16 * tps
    ch = 512
    wide = 2 * ch
    nch, nw, nb = ffl // ch, ffl // wide, dl // wide
    vmem = pl.BlockSpec(memory_space=pltpu.VMEM)
    hbm = pl.BlockSpec(memory_space=pl.ANY)
    dma = pltpu.SemaphoreType.DMA
    return pl.pallas_call(
        functools.partial(grid_kernel, tps, ch, (1, 4, 7)),
        out_shape=jax.ShapeDtypeStruct((tps, dl), BF16),
        in_specs=[hbm] * 5,
        out_specs=vmem,
        scratch_shapes=[
            pltpu.VMEM((T, dl), BF16),
            pltpu.VMEM(((nb + 2) * ffl, wide), BF16),
            pltpu.VMEM((nw, T, wide), F32),
            pltpu.VMEM((T, ffl), BF16),
            pltpu.VMEM((T, ffl), BF16),
            pltpu.VMEM((ffl,), BF16),
            pltpu.VMEM((dl,), BF16),
            pltpu.VMEM((nch, 1, ch), F32),
            pltpu.VMEM((nb, 1, wide), F32),
            pltpu.VMEM((nb, 8 * tps, wide), BF16),
            pltpu.VMEM((nb, 4 * tps, wide), BF16),
            pltpu.VMEM((nb, 3 * tps, wide), BF16),
            pltpu.VMEM((nb, 2 * tps, wide), BF16),
            pltpu.VMEM((nb, tps, wide), BF16),
            dma((3,)),
            dma((nch,)),
            dma((nb,)),
            dma((48,)),
            dma((16, 2)),
            dma((5, nch)),
            dma((5, nch)),
            dma((3, nb)),
            dma((3, nb)),
            dma((4, nb)),
            dma((4, nb)),
            dma((3, nb)),
            dma((3, nb)),
            dma((2, nb)),
            dma((nb,)),
            pltpu.SemaphoreType.REGULAR,
        ],
        compiler_params=pltpu.CompilerParams(
            collective_id=0, has_side_effects=True, vmem_limit_bytes=63 * 1024 * 1024
        ),
    )(tokens, in_weight, in_bias, out_weight, out_bias)


def solution(mesh):
    R, C, DP = mesh.shape["row"], mesh.shape["col"], mesh.shape["depth"]
    Y = C // CORES

    def body(tokens, in_weight, in_bias, out_weight, out_bias):
        if (R, C, DP) == (4, 2 * CORES, 2):
            return grid_call(tokens, in_weight, in_bias, out_weight, out_bias)
        tps, dl = tokens.shape
        ffl = in_weight.shape[1]
        T = tps * R * C
        ch = 512
        nch, nb = ffl // ch, dl // ch
        n_ag = 3 * R * Y + R
        vmem = pl.BlockSpec(memory_space=pltpu.VMEM)
        hbm = pl.BlockSpec(memory_space=pl.ANY)
        dma = pltpu.SemaphoreType.DMA
        return pl.pallas_call(
            functools.partial(general_kernel, R, C, DP, tps, nch, nb, ch),
            out_shape=jax.ShapeDtypeStruct((tps, dl), BF16),
            in_specs=[vmem, hbm, vmem, hbm, vmem],
            out_specs=vmem,
            scratch_shapes=[
                pltpu.VMEM((T, dl), BF16),
                pltpu.VMEM((nch, dl, ch), BF16),
                pltpu.VMEM((nch, T, ch), F32),
                pltpu.VMEM((nch, T, ch), BF16),
                pltpu.VMEM((DP - 1, nch, T, ch), BF16),
                pltpu.VMEM((T, ffl), BF16),
                pltpu.VMEM((nb, T, ch), F32),
                pltpu.VMEM((nb, T // CORES, ch), BF16),
                pltpu.VMEM((nb, T // CORES, ch), BF16),
                pltpu.VMEM((Y - 1, nb, R * tps, ch), BF16),
                pltpu.VMEM((Y - 1, nb, R * tps, ch), BF16),
                pltpu.VMEM((nb, R * tps, ch), F32),
                pltpu.VMEM((R - 1, nb, tps, ch), BF16),
                pltpu.VMEM((R - 1, nb, tps, ch), BF16),
                dma((nch,)),
                dma((nb,)),
                dma((n_ag,)),
                dma((R * C,)),
                dma((DP - 1, nch, 2)),
                dma((DP - 1, nch, 2)),
                dma((nb,)),
                dma((nb,)),
                dma((Y - 1, nb)),
                dma((Y - 1, nb)),
                dma((R - 1, nb)),
                dma((R - 1, nb)),
            ],
            compiler_params=pltpu.CompilerParams(
                collective_id=0, has_side_effects=True, vmem_limit_bytes=63 * 1024 * 1024
            ),
        )(tokens, in_weight, in_bias.reshape(1, ffl), out_weight, out_bias.reshape(1, dl))

    in_specs = (
        P(("row", "col"), "depth"),
        P("depth", ("row", "col")),
        P(("row", "col")),
        P(("row", "col"), "depth"),
        P("depth"),
    )
    out_specs = P(("row", "col"), "depth")
    return jax.shard_map(body, mesh=mesh, in_specs=in_specs, out_specs=out_specs, check_vma=False)
```
